256 devices in a mesh: gx: 4 (over z_hi, core), gy: 4 (over z_lo), gz: 16 (over x, y).
Axes of the slice: x: 4, y: 4, z: 8 (z_hi: 2, z_lo: 4; z = z_hi * 4 + z_lo), core: 2. Of those that a mesh axis runs over, the one named last changes fastest.
Arguments:
- charges: float32 [512, 128, 512], P('gz', 'gy', 'gx'), may hold values from -8 to 8
- kernel_taps: float32 [3, 2, 17], replicated, may hold values from 0 to 2
Outputs:
- potential: float32 [512, 128, 512], P('gz', 'gy', 'gx')
The draws below stay inside these ranges and needn't reach their ends.
All inputs are finite; a program needn't handle non-finite values.
Results may differ from the reference program's by a relative error of at most 0.0001.
Values sent between devices are 32-bit elements; how exact they have to be, the bound alone decides.
A program may use at most 128 MiB of HBM per device.

```python
import jax
import jax.numpy as jnp
from jax import lax

RADIUS = 8
TERMS = 2
LEVELS = 3
TAPS = 17
NZ = 512
NY = 128
NX = 512


def draw_kernel_taps(key, part):
    key_width = jax.random.fold_in(key, 11)
    key_scale = jax.random.fold_in(key, 23)
    fraction = jax.random.uniform(key_width, (LEVELS, TERMS), jnp.float32)
    base_width = 1.5 * 3.3 ** jnp.arange(TERMS).astype(jnp.float32)
    widths = base_width[None, :] * 2.0 ** fraction
    magnitude = jax.random.uniform(key_scale, (LEVELS, TERMS), jnp.float32, 0.5, 1.5)
    distance = (jnp.arange(TAPS) - RADIUS).astype(jnp.float32)
    profile = jnp.exp(-(distance[None, None, :] / widths[:, :, None]) ** 2)
    profile = profile / jnp.sqrt(jnp.sum(profile * profile, axis=2, keepdims=True))
    level_factor = 2.0 ** (-0.5 * jnp.arange(LEVELS).astype(jnp.float32))
    scaling = magnitude ** (1.0 / 3.0) * level_factor[:, None]
    return profile * scaling[:, :, None]


def levels(own_key, shape, cuts, smallest, high):
    loudness = 1.0
    for position, parts in cuts:
        heights = jax.random.uniform(jax.random.fold_in(jax.random.fold_in(own_key, 6), position), (parts,), jnp.float32, smallest / len(cuts), high / len(cuts))
        loudness = loudness * jnp.repeat(jnp.exp(heights), shape[position] // parts).reshape((-1,) + (1,) * (len(shape) - 1 - position))
    return loudness


def noise(stream_key, shape, width, reach, cuts=(), dtype=jnp.bfloat16):
    gain = levels(stream_key, shape, cuts, -0.22, 0.18) if cuts else 1.0
    array = jax.random.normal(stream_key, shape, jnp.float32) * width * gain
    return jnp.minimum(jnp.maximum(array, -reach), reach).astype(dtype)


def setup_inputs(seed: int = 0) -> dict:
    arg_keys = jax.random.split(jax.random.key(seed), 3)
    charges = noise(arg_keys[0], (NZ, NY, NX), 1.0, 8.0, ((0, 16), (1, 4), (2, 4)), jnp.float32)
    kernel_taps = draw_kernel_taps(jax.random.fold_in(arg_keys[2], 71), 0)
    return {"charges": charges, "kernel_taps": kernel_taps}


RESTRICT_WEIGHTS = ((-3, -0.0625), (-1, 0.5625), (0, 1.0), (1, 0.5625), (3, -0.0625))


def convolve_axis(padded, kernel_row, axis_dim, length):
    summed = kernel_row[0] * lax.slice_in_dim(padded, 0, length, axis=axis_dim)
    for offset in range(1, TAPS):
        summed = summed + kernel_row[offset] * lax.slice_in_dim(padded, offset, offset + length, axis=axis_dim)
    return summed


def level_field(grid_charges, kernel_rows):
    extent_z, extent_y, extent_x = grid_charges.shape
    padded = jnp.pad(grid_charges, RADIUS)
    result_field = jnp.zeros(grid_charges.shape, jnp.float32)
    for term_index in range(TERMS):
        smoothed = convolve_axis(padded, kernel_rows[term_index], 0, extent_z)
        smoothed = convolve_axis(smoothed, kernel_rows[term_index], 1, extent_y)
        smoothed = convolve_axis(smoothed, kernel_rows[term_index], 2, extent_x)
        result_field = result_field + smoothed
    return result_field


def restrict_axis(padded, axis_dim, margin, count):
    summed = None
    for offset, weight in RESTRICT_WEIGHTS:
        first = margin + offset
        piece = lax.slice_in_dim(padded, first, first + 2 * count - 1, stride=2, axis=axis_dim)
        summed = weight * piece if summed is None else summed + weight * piece
    return summed


def restrict_padded(padded, margin, counts):
    result_field = restrict_axis(padded, 0, margin, counts[0])
    result_field = restrict_axis(result_field, 1, margin, counts[1])
    return restrict_axis(result_field, 2, margin, counts[2])


def prolong_axis(padded, axis_dim, margin, count):
    def take(shift):
        return lax.slice_in_dim(padded, margin + shift, margin + shift + count, axis=axis_dim)
    centre = take(0)
    odd_cells = 0.5625 * (centre + take(1)) - 0.0625 * (take(-1) + take(2))
    stacked = jnp.stack([centre, odd_cells], axis=axis_dim + 1)
    new_shape = list(centre.shape)
    new_shape[axis_dim] = 2 * count
    return stacked.reshape(new_shape)


def prolong_padded(padded, margin, counts):
    result_field = prolong_axis(padded, 0, margin, counts[0])
    result_field = prolong_axis(result_field, 1, margin, counts[1])
    return prolong_axis(result_field, 2, margin, counts[2])


def restrict_grid(grid_charges):
    extent_z, extent_y, extent_x = grid_charges.shape
    return restrict_padded(jnp.pad(grid_charges, 3), 3, (extent_z // 2, extent_y // 2, extent_x // 2))


def prolong_grid(coarse_field):
    return prolong_padded(jnp.pad(coarse_field, 2), 2, coarse_field.shape)


def reference(charges, kernel_taps):
    mid_charges = restrict_grid(charges)
    coarse_charges = restrict_grid(mid_charges)
    fine_potential = level_field(charges, kernel_taps[0])
    mid_potential = level_field(mid_charges, kernel_taps[1])
    coarse_potential = level_field(coarse_charges, kernel_taps[2])
    mid_total = mid_potential + prolong_grid(coarse_potential)
    return fine_potential + prolong_grid(mid_total)
```

```python
import functools

import jax
import jax.numpy as jnp
from jax import lax
from jax.experimental import pallas as pl
from jax.experimental.pallas import tpu as pltpu
from jax.sharding import PartitionSpec as P

F32, BF16 = jnp.float32, jnp.bfloat16
MESH = pl.DeviceIdType.MESH
HI_LANE, LO_LANE = 80, 88
NOWHERE = -10000

SIZES = ((32, 32, 128), (16, 16, 64), (8, 8, 32))
LEVELS = (
    dict(planes=48, rows=48, keep=48, own=(8, 32), z={0: (8, 8, 32), 1: (32, 0, 8), -1: (8, 40, 8)},
         y={0: (8, 8, 32), 1: (32, 0, 8), -1: (8, 40, 8)}, tiles=((8, 32),), packrows=32, groups=2,
         py={0: (0, 8, 32), 1: (24, 0, 8), -1: (0, 40, 8)}, pg={0: (0, 1, 2), 1: (1, 0, 1), -1: (0, 3, 1)},
         face=(120, 0), runs=((0, 8, 0, 8), (8, 16, 1, 0), (24, 16, 2, 0), (40, 8, 3, 0))),
    dict(planes=35, rows=48, keep=48, own=(7, 21), z={0: (7, 7, 21), 1: (16, 0, 7), -1: (12, 28, 7)},
         y={0: (8, 8, 24), 1: (16, 0, 8), -1: (40, 32, 8)}, tiles=((8, 24), (40, 8)), packrows=32, groups=2,
         py={0: (0, 8, 24), 1: (8, 0, 8), -1: (24, 32, 8)}, pg={0: (0, 1, 2), 1: (0, 0, 1), -1: (0, 3, 1)},
         face=(56, 5), runs=((0, 7, 0, 9), (7, 16, 1, 0), (23, 5, 2, 0), (28, 7, 3, 5))),
    dict(planes=29, rows=40, keep=32, own=(7, 15), z={0: (7, 7, 15), 1: (8, 0, 7), -1: (14, 22, 7)},
         y={0: (8, 8, 16), 1: (8, 0, 8), -1: (32, 24, 8)}, tiles=((8, 16), (32, 8)), packrows=24, groups=1,
         py={0: (0, 8, 16), 1: (0, 0, 8), -1: (16, 24, 8)}, pg={0: (0, 1, 1), 1: (0, 0, 1), -1: (0, 2, 1)},
         face=(24, 7), runs=((0, 7, 0, 1), (7, 15, 1, 0), (22, 7, 2, 7))),
)
STEPS = tuple((dz, dy, dx) for dx in (1, -1, 0) for dy in (1, -1, 0) for dz in (1, -1, 0) if (dz, dy, dx) != (0, 0, 0))


def split(x):
    high = x.astype(BF16)
    return high, (x - high.astype(F32)).astype(BF16)


def iota(shape, axis):
    return lax.broadcasted_iota(jnp.int32, shape, axis)


def pick(condition, value, other):
    return jnp.where(condition, value, other)


def dot(a, b):
    return jnp.dot(a, b, preferred_element_type=F32)


def exact(a, b):
    return jnp.dot(a, b, preferred_element_type=F32, precision=lax.Precision.HIGHEST)


def weight(d):
    d = jnp.abs(d)
    return pick(d == 0, 1.0, pick(d == 1, 0.5625, pick(d == 3, -0.0625, 0.0))).astype(F32)


def band(diff, row):
    total = jnp.zeros(diff.shape, F32)
    for k in range(17):
        total = pick(diff == k - 8, row[k], total)
    return total


def x_coords(slot, level):
    if level == 0:
        base, hi, lo, first, tile = 128, 128, -8, 0, 128
    elif level == 1:
        base, hi, lo, first, tile = 69, 67, -10, -2, 0
    else:
        base, hi, lo, first, tile = 39, 36, -11, -3, 0
    coord = pick(slot < base, slot + first, NOWHERE)
    h, l = slot - tile - HI_LANE, slot - tile - LO_LANE
    coord = pick((h >= 0) & (h < 8), h + hi, coord)
    return pick((l >= 0) & (l < 8), l + lo, coord)


def y_coords(row, level):
    if level == 0:
        return row - 8
    if level == 1:
        coord = pick(row < 8, row - 10, pick(row < 29, row - 10, NOWHERE))
        return pick((row >= 32) & (row < 40), row - 32 + 19, coord)
    coord = pick(row < 8, row - 11, pick(row < 23, row - 11, NOWHERE))
    return pick((row >= 24) & (row < 32), row - 24 + 12, coord)


def kernel(counts, q_hbm, taps, out, *scratch):
    (e0, e1, e2, px0, px1, px2, pk0, pk1, pk2, l0h, l0l, l1h, l1l, l2h, l2l, a1, a2, f0, h1, b1, b2, c2,
     s0, s1, s2, x0h, x0l, xr1, x1h, x1l, xr2, x2h, x2l, yr1, yr2, y0, y1, y2,
     local_sem, send_sem, recv_sem) = scratch
    ext, halo, pack = (e0, e1, e2), (px0, px1, px2), (pk0, pk1, pk2)
    nz, ny, nx = counts
    gz, gy, gx = lax.axis_index("gz"), lax.axis_index("gy"), lax.axis_index("gx")

    def tap_row(level, term):
        return [taps[level, term, k] for k in range(17)]

    def neighbour(step, sign):
        dz, dy, dx = (sign * s for s in step)
        z, y, x = gz + dz, gy + dy, gx + dx
        here = None
        for d, v, n in ((dz, z, nz), (dy, y, ny), (dx, x, nx)):
            test = v < n if d > 0 else (v >= 0 if d < 0 else None)
            if test is not None:
                here = test if here is None else here & test
        return here, {"gz": z, "gy": y, "gx": x}

    load = pltpu.make_async_copy(q_hbm, e0.at[pl.ds(8, 32), pl.ds(8, 32), :], local_sem)
    load.start()

    def clear(i, _):
        zero = jnp.zeros((8, 128), F32)
        for row in range(0, 48, 8):
            e0[i, row : row + 8, :] = zero
            e0[40 + i, row : row + 8, :] = zero
        return 0

    lax.fori_loop(0, 8, clear, 0)

    def clear_sides(i, _):
        zero = jnp.zeros((8, 128), F32)
        e0[8 + i, 0:8, :] = zero
        e0[8 + i, 40:48, :] = zero
        return 0

    lax.fori_loop(0, 32, clear_sides, 0)

    def clear_planes(ref):
        def body(i, _):
            ref[i] = jnp.zeros(ref.shape[1:], F32)
            return 0

        lax.fori_loop(0, ref.shape[0], body, 0)

    clear_planes(e1)
    clear_planes(e2)
    for ref in halo:
        for side in range(2):
            for g in range(ref.shape[1]):
                ref[side, g] = jnp.zeros(ref.shape[2:], F32)

    barrier = pltpu.get_barrier_semaphore()
    for step in STEPS:
        here, device = neighbour(step, 1)

        @pl.when(here)
        def _():
            pl.semaphore_signal(barrier, inc=1, device_id=device, device_id_type=MESH)

    def pack_faces(level):
        lv, src = LEVELS[level], ext[level]
        start, planes = lv["own"]
        lane = iota((lv["packrows"], 128), 1) // 8
        for g in range(lv["groups"]):
            faces = [jnp.zeros((lv["packrows"], 128), F32) for _ in range(2)]
            for j in range(min(16, planes - 16 * g)):
                parts = [src[start + 16 * g + j, r : r + n, :] for r, n in lv["tiles"]]
                v = parts[0] if len(parts) == 1 else jnp.concatenate(parts, axis=0)
                for f in range(2):
                    faces[f] = pick(lane == j, pltpu.roll(v, (8 * j - lv["face"][f]) % 128, 1), faces[f])
            for f in range(2):
                pack[level][f, g] = faces[f]

    def copies(level):
        lv = LEVELS[level]
        result = []
        for index, step in enumerate(STEPS):
            dz, dy, dx = step
            target, device = neighbour(step, 1)
            source, _ = neighbour(step, -1)
            if dx == 0:
                z, y = lv["z"][dz], lv["y"][dy]
                src = ext[level].at[pl.ds(z[0], z[2]), pl.ds(y[0], y[2]), :]
                dst = ext[level].at[pl.ds(z[1], z[2]), pl.ds(y[1], y[2]), :]
            else:
                side = 0 if dx == 1 else 1
                z, y = lv["pg"][dz], lv["py"][dy]
                src = pack[level].at[side, pl.ds(z[0], z[2]), pl.ds(y[0], y[2]), :]
                dst = halo[level].at[side, pl.ds(z[1], z[2]), pl.ds(y[1], y[2]), :]
            copy = pltpu.make_async_remote_copy(
                src_ref=src, dst_ref=dst, send_sem=send_sem.at[level, index], recv_sem=recv_sem.at[level, index],
                device_id=device, device_id_type=MESH)
            result.append((target, source, copy))
        return result

    def send(level):
        for target, _, copy in copies(level):
            @pl.when(target)
            def _():
                copy.start()

    def receive(level):
        for _, source, copy in copies(level):
            @pl.when(source)
            def _():
                copy.wait_recv()

    def finish(level):
        for target, _, copy in copies(level):
            @pl.when(target)
            def _():
                copy.wait_send()

    def unpack(level, lh, ll):
        lv = LEVELS[level]
        rows = lv["keep"]
        lane = iota((rows, 128), 1)
        is_hi, is_lo = (lane >= HI_LANE) & (lane < HI_LANE + 8), (lane >= LO_LANE) & (lane < LO_LANE + 8)
        for first, count, g, j0 in lv["runs"]:
            for i in range(count):
                e, j = first + i, j0 + i
                low = pltpu.roll(halo[level][0, g], (LO_LANE - 8 * j) % 128, 1)
                high = pltpu.roll(halo[level][1, g], (HI_LANE - 8 * j) % 128, 1)
                v = ext[level][e, 0:rows, :]
                if level == 0:
                    side = pick(is_hi, high, pick(is_lo, low, 0.0))
                    lh[e, :, 0:128], ll[e, :, 0:128] = split(v)
                    lh[e, :, 128:256], ll[e, :, 128:256] = split(side)
                else:
                    v = pick(is_hi, high, pick(is_lo, low, v))
                    lh[e], ll[e] = split(v)

    load.wait()
    pack_faces(0)

    reach = [1 + jnp.minimum(g, 1) + jnp.minimum(n - 1 - g, 1) for g, n in ((gz, nz), (gy, ny), (gx, nx))]
    pl.semaphore_wait(barrier, reach[0] * reach[1] * reach[2] - 1)
    send(0)

    def inside(coord, g, n, count):
        return (coord + g * n >= 0) & (coord + g * n < n * count)

    for t in range(2):
        x0h[:, 128 * t : 128 * (t + 1)], x0l[:, 128 * t : 128 * (t + 1)] = split(
            band(x_coords(iota((256, 128), 0), 0) - iota((256, 128), 1), tap_row(0, t)))
    m = iota((256, 128), 1) - 2
    xr1[...] = pick((m < 67) & inside(m, gx, 64, nx), weight(x_coords(iota((256, 128), 0), 0) - 2 * m), 0.0).astype(BF16)
    c = iota((128, 128), 1) - 3
    xr2[...] = pick((c < 36) & inside(c, gx, 32, nx), weight(x_coords(iota((128, 128), 0), 1) - 2 * c), 0.0).astype(BF16)
    sq = (128, 128)
    row, col = iota(sq, 0), iota(sq, 1)
    m_col, m_row, c_col, c_row = col - 1, row - 1, col - 2, row - 2
    up1 = weight(col - 2 * m_row)
    up1 = pick(m_row < 66, up1, 0.0)
    up2 = pick((c_row < 35) & (m_col < 66) & inside(m_col, gx, 64, nx), weight(m_col - 2 * c_row), 0.0)
    up21 = exact(up2, up1)
    for t in range(2):
        k1 = pick((m_col < 66) & inside(m_col, gx, 64, nx), band(x_coords(row, 1) - m_col, tap_row(1, t)), 0.0)
        x1h[:, 128 * t : 128 * (t + 1)], x1l[:, 128 * t : 128 * (t + 1)] = split(exact(k1, up1))
        k2 = pick((c_col < 35) & inside(c_col, gx, 32, nx), band(x_coords(row, 2) - c_col, tap_row(2, t)), 0.0)
        x2h[:, 128 * t : 128 * (t + 1)], x2l[:, 128 * t : 128 * (t + 1)] = split(exact(k2, up21))

    row, col = iota((32, 128), 0), iota((32, 128), 1)
    m = pick(row < 24, row - 2, row - 24 + 3)
    yr1[...] = pick((m < 19) & inside(m, gy, 16, ny), weight(y_coords(col, 0) - 2 * m), 0.0).astype(BF16)
    row, col = iota((24, 128), 0), iota((24, 128), 1)
    c = pick(row < 16, row - 3, row - 16 + 4)
    yr2[...] = pick((c < 12) & inside(c, gy, 8, ny), weight(y_coords(col, 1) - 2 * c), 0.0).astype(BF16)

    def band_pair(coord, centre, second, level):
        rows = [jnp.where(second, taps[level, 1, k], taps[level, 0, k]) for k in range(17)]
        return band(coord - centre, rows)

    row, col = iota((32, 128), 0), iota((32, 128), 1)
    y0[0:32], y0[32:64] = split(band_pair(y_coords(pick(col >= 48, col - 48, col), 0), row, col >= 48, 0))
    m_col = col - 1
    yup1 = pick(m_col < 18, weight(row - 2 * m_col), 0.0)
    row, col = iota(sq, 0), iota(sq, 1)
    m_row, c_col, c_row = row - 1, col - 2, row - 2
    yup2 = pick((m_row < 18) & inside(m_row, gy, 16, ny) & (c_col < 11), weight(m_row - 2 * c_col), 0.0)
    k1 = band_pair(y_coords(pick(col >= 48, col - 48, col), 1), m_row, col >= 48, 1)
    k1 = pick((m_row < 18) & inside(m_row, gy, 16, ny) & (col < 96), k1, 0.0)
    y1[0:32], y1[32:64] = split(exact(yup1, k1))
    k2 = band_pair(y_coords(pick(col >= 32, col - 32, col), 2), c_row, col >= 32, 2)
    k2 = pick((c_row < 11) & inside(c_row, gy, 8, ny) & (col < 64), k2, 0.0)
    y2[0:32], y2[32:64] = split(exact(exact(yup1, yup2), k2))

    z_low = jnp.where(gz > 0, 1.0, 0.0).astype(F32)
    z_high = jnp.where(gz < nz - 1, 1.0, 0.0).astype(F32)

    def edge(v, low, high):
        n = v.shape[0]
        return jnp.concatenate([v[:low] * z_low, v[low : n - high], v[n - high :] * z_high], axis=0)

    def lanes(ref, first, count):
        return jnp.concatenate([ref[first + i] for i in range(count)], axis=1)

    def two(lh, ll, matrix):
        return dot(lh, matrix) + dot(ll, matrix)

    def three(lh, ll, high, low):
        return dot(lh, high) + dot(ll, high) + dot(lh, low)

    receive(0)
    unpack(0, l0h, l0l)

    def restrict_x(i, _):
        lh, ll = (r[pl.ds(8 * i, 8)].reshape(384, 256) for r in (l0h, l0l))
        a1[pl.ds(4 * i, 4)] = two(lh, ll, xr1[...]).reshape(4, 2, 48, 128)
        return 0

    lax.fori_loop(0, 6, restrict_x, 0)

    def restrict_z(i, _):
        rows = pl.ds(pl.multiple_of(8 * i, 8), 8)
        even, odd = a1[:, 0, rows, :], a1[:, 1, rows, :]
        v = even[2:23] + 0.5625 * (odd[1:22] + odd[2:23]) - 0.0625 * (odd[0:21] + odd[3:24])
        a2[:, rows, :] = edge(v, 2, 3)
        return 0

    lax.fori_loop(0, 6, restrict_z, 0)
    for p in range(0, 21, 7):
        high, low = split(lanes(a2, p, 7))
        v = dot(yr1[:, 0:48], high) + dot(yr1[:, 0:48], low)
        for i in range(7):
            piece = v[:, 128 * i : 128 * (i + 1)]
            e1[7 + p + i, 8:32, :] = piece[0:24]
            e1[7 + p + i, 40:48, :] = piece[24:32]
    pack_faces(1)
    send(1)

    def conv_x0(i, _):
        lh, ll = (r[pl.ds(8 * i, 8)].reshape(384, 256) for r in (l0h, l0l))
        for t in range(2):
            cols = slice(128 * t, 128 * (t + 1))
            f0[t, pl.ds(8 * i, 8)] = three(lh, ll, x0h[:, cols], x0l[:, cols]).reshape(8, 48, 128)
        return 0

    lax.fori_loop(0, 6, conv_x0, 0)

    def conv_z(field, level, t, rows, count):
        total = taps[level, t, 0] * field[t, 0:count, rows, :]
        for k in range(1, 17):
            total = total + taps[level, t, k] * field[t, k : k + count, rows, :]
        return total

    def conv_z0(i, _):
        rows = pl.ds(pl.multiple_of(8 * i, 8), 8)
        for t in range(2):
            s0[:, pl.ds(pl.multiple_of(48 * t + 8 * i, 8), 8), :] = conv_z(f0, 0, t, rows, 32)
        return 0

    lax.fori_loop(0, 6, conv_z0, 0)

    receive(1)
    unpack(1, l1h, l1l)
    l1h[35] = jnp.zeros((48, 128), BF16)
    l1l[35] = jnp.zeros((48, 128), BF16)

    def restrict_x1(i, _):
        lh, ll = (r[pl.ds(6 * i, 6)].reshape(288, 128) for r in (l1h, l1l))
        b1[pl.ds(3 * i, 3)] = two(lh, ll, xr2[...]).reshape(3, 2, 48, 128)
        return 0

    lax.fori_loop(0, 6, restrict_x1, 0)

    def restrict_z1(i, _):
        rows = pl.ds(pl.multiple_of(8 * i, 8), 8)
        even, odd = b1[:, 0, rows, :], b1[:, 1, rows, :]
        v = odd[1:16] + 0.5625 * (even[1:16] + even[2:17]) - 0.0625 * (even[0:15] + even[3:18])
        b2[:, rows, :] = edge(v, 3, 4)
        return 0

    lax.fori_loop(0, 6, restrict_z1, 0)
    for p in range(0, 15, 5):
        high, low = split(lanes(b2, p, 5))
        v = dot(yr2[:, 0:48], high) + dot(yr2[:, 0:48], low)
        for i in range(5):
            piece = v[:, 128 * i : 128 * (i + 1)]
            e2[7 + p + i, 8:24, :] = piece[0:16]
            e2[7 + p + i, 32:40, :] = piece[16:24]
    pack_faces(2)
    send(2)

    def conv_x1(i, _):
        lh, ll = (r[pl.ds(6 * i, 6)].reshape(288, 128) for r in (l1h, l1l))
        for t in range(2):
            cols = slice(128 * t, 128 * (t + 1))
            h1[t, pl.ds(6 * i, 6)] = three(lh, ll, x1h[:, cols], x1l[:, cols]).reshape(6, 48, 128)
        return 0

    lax.fori_loop(0, 6, conv_x1, 0)

    def refine(g, n):
        even = g[1 : n + 1]
        odd = 0.5625 * (even + g[2 : n + 2]) - 0.0625 * (g[0:n] + g[3 : n + 3])
        return even, odd

    def conv_z1(i, _):
        rows = pl.ds(pl.multiple_of(8 * i, 8), 8)
        for t in range(2):
            even, odd = refine(edge(conv_z(h1, 1, t, rows, 19), 1, 2), 16)
            target = pl.ds(pl.multiple_of(48 * t + 8 * i, 8), 8)
            s1[:, 0, target, :] = even
            s1[:, 1, target, :] = odd
        return 0

    lax.fori_loop(0, 6, conv_z1, 0)

    def apply_y(matrix, depth, planes):
        high, low = split(jnp.concatenate(planes, axis=1))
        both = dot(matrix[:, 0:depth], high)
        return both[0:32] + both[32:64] + dot(matrix[0:32, 0:depth], low)

    def merge(i, _):
        v = apply_y(y0, 96, [s0[4 * i + k] for k in range(4)])
        v = v + apply_y(y1, 96, [s1[2 * i + k // 2, k % 2] for k in range(4)])
        for k in range(4):
            out[4 * i + k] = v[:, 128 * k : 128 * (k + 1)]
        return 0

    lax.fori_loop(0, 8, merge, 0)

    receive(2)
    unpack(2, l2h, l2l)
    for e in range(29, 32):
        l2h[e] = jnp.zeros((32, 128), BF16)
        l2l[e] = jnp.zeros((32, 128), BF16)

    def conv_x2(i, _):
        lh, ll = (r[pl.ds(8 * i, 8)].reshape(256, 128) for r in (l2h, l2l))
        for t in range(2):
            cols = slice(128 * t, 128 * (t + 1))
            c2[t, pl.ds(8 * i, 8)] = three(lh, ll, x2h[:, cols], x2l[:, cols]).reshape(8, 32, 128)
        return 0

    lax.fori_loop(0, 4, conv_x2, 0)

    def conv_z2(i, _):
        rows = pl.ds(pl.multiple_of(8 * i, 8), 8)
        for t in range(2):
            h = edge(conv_z(c2, 2, t, rows, 13), 2, 3)
            even = h[2:11]
            odd = 0.5625 * (h[1:11] + h[2:12]) - 0.0625 * (h[0:10] + h[3:13])
            g = []
            for k in range(9):
                g += [odd[k : k + 1], even[k : k + 1]]
            even, odd = refine(edge(jnp.concatenate(g + [odd[9:10]], axis=0), 1, 2), 16)
            target = pl.ds(pl.multiple_of(32 * t + 8 * i, 8), 8)
            s2[:, 0, target, :] = even
            s2[:, 1, target, :] = odd
        return 0

    lax.fori_loop(0, 4, conv_z2, 0)

    def add_coarse(i, _):
        v = apply_y(y2, 64, [s2[2 * i + k // 2, k % 2] for k in range(4)])
        for k in range(4):
            out[4 * i + k] = out[4 * i + k] + v[:, 128 * k : 128 * (k + 1)]
        return 0

    lax.fori_loop(0, 8, add_coarse, 0)

    for level in range(3):
        finish(level)


def solution(mesh):
    counts = tuple(mesh.shape[a] for a in ("gz", "gy", "gx"))

    def local(charges, kernel_taps):
        vm = pltpu.VMEM
        scratch = [
            vm((48, 48, 128), F32), vm((35, 48, 128), F32), vm((29, 40, 128), F32),
            vm((2, 4, 48, 128), F32), vm((2, 4, 48, 128), F32), vm((2, 3, 32, 128), F32),
            vm((2, 2, 32, 128), F32), vm((2, 2, 32, 128), F32), vm((2, 1, 24, 128), F32),
            vm((48, 48, 256), BF16), vm((48, 48, 256), BF16),
            vm((36, 48, 128), BF16), vm((36, 48, 128), BF16),
            vm((32, 32, 128), BF16), vm((32, 32, 128), BF16),
            vm((24, 2, 48, 128), F32), vm((21, 48, 128), F32),
            vm((2, 48, 48, 128), F32), vm((2, 36, 48, 128), F32),
            vm((18, 2, 48, 128), F32), vm((15, 48, 128), F32), vm((2, 32, 32, 128), F32),
            vm((32, 96, 128), F32), vm((16, 2, 96, 128), F32), vm((16, 2, 64, 128), F32),
            vm((256, 256), BF16), vm((256, 256), BF16), vm((256, 128), BF16),
            vm((128, 256), BF16), vm((128, 256), BF16), vm((128, 128), BF16),
            vm((128, 256), BF16), vm((128, 256), BF16),
            vm((32, 128), BF16), vm((24, 128), BF16),
            vm((64, 128), BF16), vm((64, 128), BF16), vm((64, 128), BF16),
            pltpu.SemaphoreType.DMA, pltpu.SemaphoreType.DMA((3, 26)), pltpu.SemaphoreType.DMA((3, 26)),
        ]
        return pl.pallas_call(
            functools.partial(kernel, counts),
            out_shape=jax.ShapeDtypeStruct((32, 32, 128), F32),
            in_specs=[pl.BlockSpec(memory_space=pl.ANY), pl.BlockSpec(memory_space=pltpu.SMEM)],
            out_specs=pl.BlockSpec(memory_space=pltpu.VMEM),
            scratch_shapes=scratch,
            compiler_params=pltpu.CompilerParams(
                collective_id=0, has_side_effects=True, vmem_limit_bytes=56 * 1024 * 1024),
        )(charges, kernel_taps)

    return jax.shard_map(
        local, mesh=mesh, in_specs=(P("gz", "gy", "gx"), P()), out_specs=P("gz", "gy", "gx"), check_vma=False)
```

```python
import functools

import jax
import jax.numpy as jnp
from jax import lax
from jax.experimental import pallas as pl
from jax.experimental.pallas import tpu as pltpu
from jax.sharding import PartitionSpec as P

F32, BF16 = jnp.float32, jnp.bfloat16
MESH = pl.DeviceIdType.MESH
NOWHERE = -10000

LEVELS = (
    dict(keep=48, own=(8, 32), z={0: (8, 8, 32), 1: (32, 0, 8), -1: (8, 40, 8)},
         y={0: (8, 8, 32), 1: (32, 0, 8), -1: (8, 40, 8)}, tiles=((8, 32),), packrows=32, groups=2, lanes=(80, 88),
         py={0: (0, 8, 32), 1: (24, 0, 8), -1: (0, 40, 8)}, pg={0: (0, 1, 2), 1: (1, 0, 1), -1: (0, 3, 1)},
         face=(120, 0), runs=((0, 8, 0, 8), (8, 16, 1, 0), (24, 16, 2, 0), (40, 8, 3, 0))),
    dict(keep=40, own=(7, 21), z={0: (7, 7, 21), 1: (16, 0, 7), -1: (12, 28, 7)},
         y={0: (8, 8, 24), 1: (16, 0, 8), -1: (40, 32, 8)}, tiles=((8, 24), (40, 8)), packrows=32, groups=2, lanes=(80, 88),
         py={0: (0, 8, 24), 1: (8, 0, 8), -1: (24, 32, 8)}, pg={0: (0, 1, 2), 1: (0, 0, 1), -1: (0, 3, 1)},
         face=(56, 5), runs=((0, 7, 0, 9), (7, 16, 1, 0), (23, 5, 2, 0), (28, 7, 3, 5))),
    dict(keep=32, own=(7, 15), z={0: (7, 7, 15), 1: (8, 0, 7), -1: (14, 22, 7)},
         y={0: (8, 8, 16), 1: (8, 0, 8), -1: (32, 24, 8)}, tiles=((8, 16), (32, 8)), packrows=24, groups=1, lanes=(40, 48),
         py={0: (0, 8, 16), 1: (0, 0, 8), -1: (16, 24, 8)}, pg={0: (0, 1, 1), 1: (0, 0, 1), -1: (0, 2, 1)},
         face=(24, 7), runs=((0, 7, 0, 1), (7, 15, 1, 0), (22, 7, 2, 7))),
)
STEPS = tuple((dz, dy, dx) for dx in (1, -1, 0) for dy in (1, -1, 0) for dz in (1, -1, 0) if (dz, dy, dx) != (0, 0, 0))


def split(x):
    high = x.astype(BF16)
    return high, (x - high.astype(F32)).astype(BF16)


def iota(shape, axis):
    return lax.broadcasted_iota(jnp.int32, shape, axis)


def pick(condition, value, other):
    return jnp.where(condition, value, other)


def dot(a, b):
    return jnp.dot(a, b, preferred_element_type=F32)


def exact(a, b):
    return jnp.dot(a, b, preferred_element_type=F32, precision=lax.Precision.HIGHEST)


def weight(d):
    d = jnp.abs(d)
    return pick(d == 0, 1.0, pick(d == 1, 0.5625, pick(d == 3, -0.0625, 0.0))).astype(F32)


def band(diff, row):
    total = jnp.zeros(diff.shape, F32)
    for k in range(17):
        total = pick(diff == k - 8, row[k], total)
    return total


def x_coords(slot, level):
    if level == 0:
        base, hi, lo, first, tile = 128, 128, -8, 0, 128
    elif level == 1:
        base, hi, lo, first, tile = 69, 67, -10, -2, 0
    else:
        base, hi, lo, first, tile = 39, 36, -11, -3, 0
    coord = pick(slot < base, slot + first, NOWHERE)
    h, l = slot - tile - LEVELS[level]["lanes"][0], slot - tile - LEVELS[level]["lanes"][1]
    coord = pick((h >= 0) & (h < 8), h + hi, coord)
    return pick((l >= 0) & (l < 8), l + lo, coord)


def y_coords(row, level):
    if level == 0:
        return row - 8
    if level == 1:
        coord = pick(row < 8, row - 10, pick(row < 29, row - 10, NOWHERE))
        return pick((row >= 32) & (row < 40), row - 32 + 19, coord)
    coord = pick(row < 8, row - 11, pick(row < 23, row - 11, NOWHERE))
    return pick((row >= 24) & (row < 32), row - 24 + 12, coord)


def kernel(counts, q_hbm, taps_hbm, out, *scratch):
    (e0, e1, e2, px0, px1, px2, pk0, pk1, pk2, side, v1, v2, r0, r1, f0, s0, z1, q1h, q1l, t1, z2, t2,
     x0, xr1, x1, xr2, x2, yr1, yr2, y0, y1, y2, taps, local_sem, taps_sem, send_sem, recv_sem) = scratch
    ext, halo, pack = (e0, e1, e2), (px0, px1, px2), (pk0, pk1, pk2)
    nz, ny, nx = counts
    gz, gy, gx = lax.axis_index("gz"), lax.axis_index("gy"), lax.axis_index("gx")

    def neighbour(step, sign):
        dz, dy, dx = (sign * s for s in step)
        z, y, x = gz + dz, gy + dy, gx + dx
        here = None
        for d, v, n in ((dz, z, nz), (dy, y, ny), (dx, x, nx)):
            test = v < n if d > 0 else (v >= 0 if d < 0 else None)
            if test is not None:
                here = test if here is None else here & test
        return here, {"gz": z, "gy": y, "gx": x}

    load = pltpu.make_async_copy(q_hbm, e0.at[pl.ds(8, 32), pl.ds(8, 32), :], local_sem)
    load.start()
    load_taps = pltpu.make_async_copy(taps_hbm, taps, taps_sem)
    load_taps.start()

    barrier = pltpu.get_barrier_semaphore()
    for step in STEPS:
        here, device = neighbour(step, 1)

        @pl.when(here)
        def _():
            pl.semaphore_signal(barrier, inc=1, device_id=device, device_id_type=MESH)

    def places(level, step):
        lv = LEVELS[level]
        dz, dy, dx = step
        if dx == 0:
            z, y = lv["z"][dz], lv["y"][dy]
            src = ext[level].at[pl.ds(z[0], z[2]), pl.ds(y[0], y[2]), :]
            dst = ext[level].at[pl.ds(z[1], z[2]), pl.ds(y[1], y[2]), :]
        else:
            face = 0 if dx == 1 else 1
            z, y = lv["pg"][dz], lv["py"][dy]
            src = pack[level].at[face, pl.ds(z[0], z[2]), pl.ds(y[0], y[2]), :]
            dst = halo[level].at[face, pl.ds(z[1], z[2]), pl.ds(y[1], y[2]), :]
        return src, dst

    for level in range(3):
        for step in STEPS:
            source, _ = neighbour(step, -1)
            _, dst = places(level, step)

            @pl.when(jnp.logical_not(source))
            def _():
                dst[...] = jnp.zeros(dst.shape, F32)

    def pack_faces(level):
        lv, src = LEVELS[level], ext[level]
        start, planes = lv["own"]
        lane = iota((lv["packrows"], 128), 1) // 8
        for g in range(lv["groups"]):
            faces = [jnp.zeros((lv["packrows"], 128), F32) for _ in range(2)]
            for j in range(min(16, planes - 16 * g)):
                parts = [src[start + 16 * g + j, r : r + n, :] for r, n in lv["tiles"]]
                v = parts[0] if len(parts) == 1 else jnp.concatenate(parts, axis=0)
                for f in range(2):
                    faces[f] = pick(lane == j, pltpu.roll(v, (8 * j - lv["face"][f]) % 128, 1), faces[f])
            for f in range(2):
                pack[level][f, g] = faces[f]

    def copies(level):
        result = []
        for index, step in enumerate(STEPS):
            target, device = neighbour(step, 1)
            source, _ = neighbour(step, -1)
            src, dst = places(level, step)
            copy = pltpu.make_async_remote_copy(
                src_ref=src, dst_ref=dst, send_sem=send_sem.at[level, index], recv_sem=recv_sem.at[level, index],
                device_id=device, device_id_type=MESH)
            result.append((target, source, copy))
        return result

    def send(level):
        for target, _, copy in copies(level):
            @pl.when(target)
            def _():
                copy.start()

    def receive(level):
        for _, source, copy in copies(level):
            @pl.when(source)
            def _():
                copy.wait_recv()

    def finish(level):
        for target, _, copy in copies(level):
            @pl.when(target)
            def _():
                copy.wait_send()

    def unpack(level, target):
        lv = LEVELS[level]
        rows = lv["keep"]
        lane = iota((rows, 128), 1)
        hi, lo = lv["lanes"]
        is_hi, is_lo = (lane >= hi) & (lane < hi + 8), (lane >= lo) & (lane < lo + 8)
        for first, count, g, j0 in lv["runs"]:
            for i in range(count):
                e, j = first + i, j0 + i
                low = pltpu.roll(halo[level][0, g], (lo - 8 * j) % 128, 1)
                high = pltpu.roll(halo[level][1, g], (hi - 8 * j) % 128, 1)
                own = 0.0 if level == 0 else ext[level][e, 0:rows, :]
                v = pick(is_hi, high, pick(is_lo, low, own))
                target[e] = pick(lane < 64, v, pltpu.roll(v, 64, 1)) if level == 2 else v

    load.wait()
    pack_faces(0)
    reach = [1 + jnp.minimum(g, 1) + jnp.minimum(n - 1 - g, 1) for g, n in ((gz, nz), (gy, ny), (gx, nx))]
    pl.semaphore_wait(barrier, reach[0] * reach[1] * reach[2] - 1)
    send(0)

    load_taps.wait()

    def tap_row(level, term):
        return [taps[level, term, k] for k in range(17)]

    def tap_pair(level, second):
        return [jnp.where(second, taps[level, 1, k], taps[level, 0, k]) for k in range(17)]

    def inside(coord, g, n, count):
        return (coord + g * n >= 0) & (coord + g * n < n * count)

    for t in range(2):
        high, low = split(band(x_coords(iota((256, 128), 0), 0) - iota((256, 128), 1), tap_row(0, t)))
        cols = slice(128 * t, 128 * (t + 1))
        x0[0:256, cols], x0[256:512, cols], x0[512:768, cols] = high, high, low
    m = iota((256, 128), 1) - 2
    high = pick((m < 67) & inside(m, gx, 64, nx), weight(x_coords(iota((256, 128), 0), 0) - 2 * m), 0.0).astype(BF16)
    xr1[0:256], xr1[256:512] = high, high
    c = iota((128, 128), 1) - 3
    high = pick((c < 36) & inside(c, gx, 32, nx), weight(x_coords(iota((128, 128), 0), 1) - 2 * c), 0.0).astype(BF16)
    xr2[0:128], xr2[128:256] = high, high
    sq = (128, 128)
    row, col = iota(sq, 0), iota(sq, 1)
    m_col, m_row, c_col, c_row = col - 1, row - 1, col - 2, row - 2
    up1 = pick(m_row < 66, weight(col - 2 * m_row), 0.0)
    up2 = pick((c_row < 35) & (m_col < 66) & inside(m_col, gx, 64, nx), weight(m_col - 2 * c_row), 0.0)
    up21 = exact(up2, up1)
    for t in range(2):
        k1 = pick((m_col < 66) & inside(m_col, gx, 64, nx), band(x_coords(row, 1) - m_col, tap_row(1, t)), 0.0)
        high, low = split(exact(k1, up1))
        for first, part in ((0, high), (256, high), (512, low)):
            x1[first + 128 * t : first + 128 * (t + 1)] = part
    k2 = band(x_coords(pick(row < 64, row, row - 64), 2) - c_col, tap_pair(2, row >= 64))
    k2 = pick((c_col < 35) & inside(c_col, gx, 32, nx), k2, 0.0)
    high, low = split(exact(k2, up21))
    x2[0:128], x2[128:256], x2[256:384] = high, high, low

    row, col = iota((32, 128), 0), iota((32, 128), 1)
    m = pick(row < 24, row - 2, row - 24 + 3)
    yr1[...] = pick((m < 19) & inside(m, gy, 16, ny), weight(y_coords(col, 0) - 2 * m), 0.0).astype(BF16)
    y0[0:32], y0[32:64] = split(band(y_coords(pick(col >= 48, col - 48, col), 0) - row, tap_pair(0, col >= 48)))
    m_col = col - 1
    yup1 = pick(m_col < 18, weight(row - 2 * m_col), 0.0)
    row, col = iota((24, 128), 0), iota((24, 128), 1)
    c = pick(row < 16, row - 3, row - 16 + 4)
    yr2[...] = pick((c < 12) & inside(c, gy, 8, ny), weight(y_coords(col, 1) - 2 * c), 0.0).astype(BF16)
    row, col = iota(sq, 0), iota(sq, 1)
    m_row, c_col, c_row = row - 1, col - 2, row - 2
    yup2 = pick((m_row < 18) & inside(m_row, gy, 16, ny) & (c_col < 11), weight(m_row - 2 * c_col), 0.0)
    yup21 = exact(yup1, yup2)
    for t in range(2):
        k1 = pick((m_row < 18) & inside(m_row, gy, 16, ny), band(y_coords(col, 1) - m_row, tap_row(1, t)), 0.0)
        y1[64 * t : 64 * t + 32], y1[64 * t + 32 : 64 * t + 64] = split(exact(yup1, k1))
        k2 = pick((c_row < 11) & inside(c_row, gy, 8, ny), band(y_coords(col, 2) - c_row, tap_row(2, t)), 0.0)
        y2[32 * t : 32 * t + 32], y2[64 + 32 * t : 96 + 32 * t] = split(exact(yup21, k2))

    z_low = jnp.where(gz > 0, 1.0, 0.0).astype(F32)
    z_high = jnp.where(gz < nz - 1, 1.0, 0.0).astype(F32)

    def edge(v, low, high):
        n = v.shape[0]
        return jnp.concatenate([v[:low] * z_low, v[low : n - high], v[n - high :] * z_high], axis=0)

    def join(parts, axis):
        return parts[0] if len(parts) == 1 else jnp.concatenate(parts, axis=axis)

    def pieces(v, count):
        return [v[:, 128 * i : 128 * (i + 1)] for i in range(count)]

    receive(0)
    unpack(0, side)

    def restrict_z(i, _):
        rows = pl.ds(pl.multiple_of(8 * i, 8), 8)

        def line(ref):
            even, odd = (jnp.concatenate([ref[2 * k + h : 2 * k + h + 1, rows, :] for k in range(24)], axis=0) for h in range(2))
            v = even[2:23] + 0.5625 * (odd[1:22] + odd[2:23]) - 0.0625 * (odd[0:21] + odd[3:24])
            return edge(v, 2, 3)

        r0[:, rows, 0:128] = line(e0)
        r0[:, rows, 128:256] = line(side)
        return 0

    lax.fori_loop(0, 6, restrict_z, 0)
    for p in range(0, 21, 7):
        high, low = split(join([r0[p + i, :, 0:128] for i in range(7)] + [r0[p + i, :, 128:256] for i in range(7)], 1))
        v = pieces(dot(yr1[:, 0:48], high) + dot(yr1[:, 0:48], low), 14)
        v = join([join([v[i], v[7 + i]], 1) for i in range(7)], 0)
        v = dot(join(split(v), 1), xr1[...]).reshape(7, 32, 128)
        for i in range(7):
            e1[7 + p + i, 8:32, :] = v[i, 0:24]
            e1[7 + p + i, 40:48, :] = v[i, 24:32]
    pack_faces(1)
    send(1)

    def conv_x0(i, _):
        planes = pl.ds(8 * i, 8)
        own_high, own_low = split(e0[planes].reshape(384, 128))
        side_high, side_low = split(side[planes].reshape(384, 128))
        left = join([own_high, side_high, own_low, side_low, own_high, side_high], 1)
        v = dot(left, x0[...])
        for t in range(2):
            f0[t, planes] = v[:, 128 * t : 128 * (t + 1)].reshape(8, 48, 128)
        return 0

    lax.fori_loop(0, 6, conv_x0, 0)

    def conv_z(field, row, count):
        total = row[0] * field(0, count)
        for k in range(1, 17):
            total = total + row[k] * field(k, count)
        return total

    def conv_z0(i, _):
        rows = pl.ds(pl.multiple_of(8 * i, 8), 8)
        for t in range(2):
            target = pl.ds(pl.multiple_of(48 * t + 8 * i, 8), 8)
            s0[:, target, :] = conv_z(lambda k, n: f0[t, k : k + n, rows, :], tap_row(0, t), 32)
        return 0

    lax.fori_loop(0, 6, conv_z0, 0)

    def fine_y(i, _):
        high, low = split(join([s0[4 * i + k] for k in range(4)], 1))
        both = dot(y0[:, 0:96], high)
        v = pieces(both[0:32] + both[32:64] + dot(y0[0:32, 0:96], low), 4)
        for k in range(4):
            out[2 * i + k // 2, k % 2] = v[k]
        return 0

    lax.fori_loop(0, 8, fine_y, 0)

    receive(1)
    unpack(1, v1)

    def restrict_z1(i, _):
        rows = pl.ds(pl.multiple_of(8 * i, 8), 8)
        even = jnp.concatenate([v1[2 * k : 2 * k + 1, rows, :] for k in range(18)], axis=0)
        odd = jnp.concatenate([v1[2 * k + 1 : 2 * k + 2, rows, :] for k in range(17)], axis=0)
        v = odd[1:16] + 0.5625 * (even[1:16] + even[2:17]) - 0.0625 * (even[0:15] + even[3:18])
        r1[:, rows, :] = edge(v, 3, 4)
        return 0

    lax.fori_loop(0, 5, restrict_z1, 0)
    high, low = split(join([r1[p] for p in range(15)], 1))
    v = dot(yr2[:, 0:40], high) + dot(yr2[:, 0:40], low)
    v = dot(join(split(join(pieces(v, 15), 0)), 1), xr2[...]).reshape(15, 24, 128)
    for p in range(15):
        e2[7 + p, 8:24, :] = v[p, 0:16]
        e2[7 + p, 32:40, :] = v[p, 16:24]
    pack_faces(2)
    send(2)

    def conv_z1(i, _):
        rows = pl.ds(pl.multiple_of(8 * i, 8), 8)
        for t in range(2):
            z1[t, :, rows, :] = edge(conv_z(lambda k, n: v1[k : k + n, rows, :], tap_row(1, t), 19), 1, 2)
        return 0

    lax.fori_loop(0, 5, conv_z1, 0)
    for t in range(2):
        for p, n in ((0, 7), (7, 6), (13, 6)):
            high, low = split(join([z1[t, p + i] for i in range(n)], 1))
            both = dot(y1[64 * t : 64 * t + 64, 0:40], high)
            v = both[0:32] + both[32:64] + dot(y1[64 * t : 64 * t + 32, 0:40], low)
            for i, piece in enumerate(pieces(v, n)):
                q1h[p + i, :, 128 * t : 128 * (t + 1)], q1l[p + i, :, 128 * t : 128 * (t + 1)] = split(piece)
    for p, n in ((0, 7), (7, 6), (13, 6)):
        high, low = (r[p : p + n].reshape(32 * n, 256) for r in (q1h, q1l))
        t1[p : p + n] = dot(join([high, low, high], 1), x1[...]).reshape(n, 32, 128)

    def refine(g, n):
        even = g[1 : n + 1]
        return even, 0.5625 * (even + g[2 : n + 2]) - 0.0625 * (g[0:n] + g[3 : n + 3])

    def add_middle(i, _):
        rows = pl.ds(pl.multiple_of(8 * i, 8), 8)
        for h, v in enumerate(refine(t1[:, rows, :], 16)):
            out[:, h, rows, :] = out[:, h, rows, :] + v
        return 0

    lax.fori_loop(0, 4, add_middle, 0)

    for level in range(3):
        finish(level)
    receive(2)
    unpack(2, v2)

    first_term = iota((8, 128), 1) < 64

    def conv_z2(i, _):
        rows = pl.ds(pl.multiple_of(8 * i, 8), 8)
        row = [v[None] for v in tap_pair(2, jnp.logical_not(first_term))]
        z2[:, rows, :] = edge(conv_z(lambda k, n: v2[k : k + n, rows, :], row, 13), 2, 3)
        return 0

    lax.fori_loop(0, 4, conv_z2, 0)
    lane = iota((32, 128), 1)
    for p, n in ((0, 7), (7, 6)):
        high, low = split(join([z2[p + i] for i in range(n)], 1))
        both, rest = dot(y2[:, 0:32], high), dot(y2[0:64, 0:32], low)
        terms = [pieces(both[32 * t : 32 * t + 32] + both[64 + 32 * t : 96 + 32 * t] + rest[32 * t : 32 * t + 32], n) for t in range(2)]
        high, low = split(join([pick(lane < 64, a, b) for a, b in zip(*terms)], 0))
        t2[p : p + n] = dot(join([high, low, high], 1), x2[...]).reshape(n, 32, 128)

    def add_coarse(i, _):
        rows = pl.ds(pl.multiple_of(8 * i, 8), 8)
        h = t2[:, rows, :]
        even = h[2:11]
        odd = 0.5625 * (h[1:11] + h[2:12]) - 0.0625 * (h[0:10] + h[3:13])
        g = []
        for k in range(9):
            g += [odd[k : k + 1], even[k : k + 1]]
        g = edge(jnp.concatenate(g + [odd[9:10]], axis=0), 1, 2)
        for h, v in enumerate(refine(g, 16)):
            out[:, h, rows, :] = out[:, h, rows, :] + v
        return 0

    lax.fori_loop(0, 4, add_coarse, 0)


def solution(mesh):
    counts = tuple(mesh.shape[a] for a in ("gz", "gy", "gx"))

    def local(charges, kernel_taps):
        vm = pltpu.VMEM
        scratch = [
            vm((48, 48, 128), F32), vm((35, 48, 128), F32), vm((29, 40, 128), F32),
            vm((2, 4, 48, 128), F32), vm((2, 4, 40, 128), F32), vm((2, 3, 32, 128), F32),
            vm((2, 2, 32, 128), F32), vm((2, 2, 32, 128), F32), vm((2, 1, 24, 128), F32),
            vm((48, 48, 128), F32), vm((35, 40, 128), F32), vm((29, 32, 128), F32),
            vm((21, 48, 256), F32), vm((15, 40, 128), F32), vm((2, 48, 48, 128), F32), vm((32, 96, 128), F32),
            vm((2, 19, 40, 128), F32), vm((19, 32, 256), BF16), vm((19, 32, 256), BF16), vm((19, 32, 128), F32),
            vm((13, 32, 128), F32), vm((13, 32, 128), F32),
            vm((768, 256), BF16), vm((512, 128), BF16), vm((768, 128), BF16), vm((256, 128), BF16), vm((384, 128), BF16),
            vm((32, 128), BF16), vm((24, 128), BF16), vm((64, 128), BF16), vm((128, 128), BF16), vm((128, 128), BF16),
            pltpu.SMEM((3, 2, 17), F32),
            pltpu.SemaphoreType.DMA, pltpu.SemaphoreType.DMA, pltpu.SemaphoreType.DMA((3, 26)), pltpu.SemaphoreType.DMA((3, 26)),
        ]
        result = pl.pallas_call(
            functools.partial(kernel, counts),
            out_shape=jax.ShapeDtypeStruct((16, 2, 32, 128), F32),
            in_specs=[pl.BlockSpec(memory_space=pltpu.HBM)] * 2,
            out_specs=pl.BlockSpec(memory_space=pltpu.VMEM),
            scratch_shapes=scratch,
            compiler_params=pltpu.CompilerParams(
                collective_id=0, has_side_effects=True, vmem_limit_bytes=26 * 1024 * 1024),
        )(*(pltpu.with_memory_space_constraint(a, pltpu.HBM) for a in (charges, kernel_taps)))
        return result.reshape(32, 32, 128)

    return jax.shard_map(
        local, mesh=mesh, in_specs=(P("gz", "gy", "gx"), P()), out_specs=P("gz", "gy", "gx"), check_vma=False)
```

```python
import functools

import jax
import jax.numpy as jnp
from jax import lax
from jax.experimental import pallas as pl
from jax.experimental.pallas import tpu as pltpu
from jax.sharding import PartitionSpec as P

F32, BF16 = jnp.float32, jnp.bfloat16
MESH = pl.DeviceIdType.MESH
NOWHERE = -10000

LEVELS = (
    dict(keep=48, own=(8, 32), z={0: (8, 8, 32), 1: (32, 0, 8), -1: (8, 40, 8)},
         y={0: (8, 8, 32), 1: (32, 0, 8), -1: (8, 40, 8)}, tiles=((8, 32),), packrows=32, groups=(0, 16), width=8,
         py={0: (0, 8, 32), 1: (24, 0, 8), -1: (0, 40, 8)}, pg={0: (0, 1, 2), 1: (1, 0, 1), -1: (0, 3, 1)},
         face=(120, 0), hi=(80, 8, 0), lo=(88, 8, 0), runs=((0, 8, 0, 8), (8, 16, 1, 0), (24, 16, 2, 0), (40, 8, 3, 0))),
    dict(keep=40, own=(7, 21), z={0: (7, 7, 21), 1: (16, 0, 7), -1: (12, 28, 7)},
         y={0: (8, 8, 24), 1: (16, 0, 8), -1: (40, 32, 8)}, tiles=((8, 24), (40, 8)), packrows=32, groups=(0, 8, 16, 4), width=16,
         py={0: (0, 8, 24), 1: (8, 0, 8), -1: (24, 32, 8)}, pg={0: (0, 1, 3), 1: (1, 0, 1), -1: (3, 4, 1)},
         face=(51, 0), hi=(80, 16, 0), lo=(96, 16, 0), runs=((0, 7, 0, 1), (7, 8, 1, 0), (15, 8, 2, 0), (23, 5, 3, 0), (28, 7, 4, 1))),
    dict(keep=32, own=(7, 15), z={0: (3, 3, 6), 1: (4, 0, 3), -1: (6, 9, 3)},
         y={0: (8, 8, 16), 1: (8, 0, 8), -1: (32, 24, 8)}, tiles=((8, 16), (32, 8)), packrows=24, groups=(0, 8, 7), width=16,
         py={0: (0, 8, 16), 1: (0, 0, 8), -1: (16, 24, 8)}, pg={0: (0, 1, 2), 1: (0, 0, 1), -1: (2, 3, 1)},
         face=(21, 0), hi=(37, 13, 0), lo=(50, 13, 3), runs=((0, 7, 0, 1), (7, 8, 1, 0), (15, 7, 2, 0), (22, 7, 3, 0))),
)
STEPS = tuple((dz, dy, dx) for dx in (1, -1, 0) for dy in (1, -1, 0) for dz in (1, -1, 0) if (dz, dy, dx) != (0, 0, 0))


def coarse_place(e):
    if e < 7:
        return e // 3, 42 * (e % 3)
    if e < 22:
        return 3 + (e - 5) // 3, 42 * ((e - 5) % 3)
    return 9 + (e - 22) // 3, 42 * ((e - 22) % 3)


def split(x):
    high = x.astype(BF16)
    return high, (x - high.astype(F32)).astype(BF16)


def iota(shape, axis):
    return lax.broadcasted_iota(jnp.int32, shape, axis)


def pick(condition, value, other):
    return jnp.where(condition, value, other)


def dot(a, b):
    return jnp.dot(a, b, preferred_element_type=F32)


def join(parts, axis):
    return parts[0] if len(parts) == 1 else jnp.concatenate(parts, axis=axis)


def exact(a, b):
    return jnp.dot(a, b, preferred_element_type=F32, precision=lax.Precision.HIGHEST)


def weight(d):
    d = jnp.abs(d)
    return pick(d == 0, 1.0, pick(d == 1, 0.5625, pick(d == 3, -0.0625, 0.0))).astype(F32)


def band(diff, row):
    total = jnp.zeros(diff.shape, F32)
    for k in range(17):
        total = pick(diff == k - 8, row[k], total)
    return total


def x_coords(slot, level):
    base, first, high, low, tile = ((128, 0, 128, -8, 128), (67, -1, 63, -14, 0), (37, -2, 30, -10, 0))[level]
    coord = pick(slot < base, slot + first, NOWHERE)
    for (start, count, _), value in ((LEVELS[level]["hi"], high), (LEVELS[level]["lo"], low)):
        k = slot - tile - start
        coord = pick((k >= 0) & (k < count), k + value, coord)
    return coord


def y_coords(row, level):
    if level == 0:
        return row - 8
    if level == 1:
        coord = pick(row < 8, row - 10, pick(row < 29, row - 10, NOWHERE))
        return pick((row >= 32) & (row < 40), row - 32 + 19, coord)
    coord = pick(row < 8, row - 11, pick(row < 23, row - 11, NOWHERE))
    return pick((row >= 24) & (row < 32), row - 24 + 12, coord)


def kernel(counts, q_hbm, taps_hbm, out, *scratch):
    (e0, e1, e2, px0, px1, px2, pk0, pk1, pk2, side, v1, v2, r0, r1, f0, s0, z1, q1h, q1l, t1, z2, t2,
     x0, xr1, x1, xr2, x2, yr1, yr2, y0, y1, y2, taps, local_sem, taps_sem, send_sem, recv_sem) = scratch
    ext, halo, pack = (e0, e1, e2), (px0, px1, px2), (pk0, pk1, pk2)
    nz, ny, nx = counts
    gz, gy, gx = lax.axis_index("gz"), lax.axis_index("gy"), lax.axis_index("gx")

    def neighbour(step, sign):
        dz, dy, dx = (sign * s for s in step)
        z, y, x = gz + dz, gy + dy, gx + dx
        here = None
        for d, v, n in ((dz, z, nz), (dy, y, ny), (dx, x, nx)):
            test = v < n if d > 0 else (v >= 0 if d < 0 else None)
            if test is not None:
                here = test if here is None else here & test
        return here, {"gz": z, "gy": y, "gx": x}

    load = pltpu.make_async_copy(q_hbm, e0.at[pl.ds(8, 32), pl.ds(8, 32), :], local_sem)
    load.start()
    load_taps = pltpu.make_async_copy(taps_hbm, taps, taps_sem)
    load_taps.start()

    barrier = pltpu.get_barrier_semaphore()
    for step in STEPS:
        here, device = neighbour(step, 1)

        @pl.when(here)
        def _():
            pl.semaphore_signal(barrier, inc=1, device_id=device, device_id_type=MESH)

    def places(level, step):
        lv = LEVELS[level]
        dz, dy, dx = step
        if dx == 0:
            z, y = lv["z"][dz], lv["y"][dy]
            src = ext[level].at[pl.ds(z[0], z[2]), pl.ds(y[0], y[2]), :]
            dst = ext[level].at[pl.ds(z[1], z[2]), pl.ds(y[1], y[2]), :]
        else:
            face = 0 if dx == 1 else 1
            z, y = lv["pg"][dz], lv["py"][dy]
            src = pack[level].at[face, pl.ds(z[0], z[2]), pl.ds(y[0], y[2]), :]
            dst = halo[level].at[face, pl.ds(z[1], z[2]), pl.ds(y[1], y[2]), :]
        return src, dst

    for level in range(3):
        for step in STEPS:
            source, _ = neighbour(step, -1)
            _, dst = places(level, step)

            @pl.when(jnp.logical_not(source))
            def _():
                dst[...] = jnp.zeros(dst.shape, F32)

    def pack_faces(level):
        lv, src, width = LEVELS[level], ext[level], LEVELS[level]["width"]
        start, planes = lv["own"]
        lane = iota((lv["packrows"], 128), 1) // width
        for g, offset in enumerate(lv["groups"]):
            faces = [jnp.zeros((lv["packrows"], 128), F32) for _ in range(2)]
            for j in range(min(128 // width, planes - offset)):
                e, shift = start + offset + j, width * j
                if level == 2:
                    e, first = coarse_place(e)
                    shift -= first
                v = join([src[e, r : r + n, :] for r, n in lv["tiles"]], 0)
                for f in range(2):
                    faces[f] = pick(lane == j, pltpu.roll(v, (shift - lv["face"][f]) % 128, 1), faces[f])
            for f in range(2):
                pack[level][f, g] = faces[f]

    def copies(level, across):
        result = []
        for index, step in enumerate(STEPS):
            if across is not None and (step[2] != 0) != across:
                continue
            target, device = neighbour(step, 1)
            source, _ = neighbour(step, -1)
            src, dst = places(level, step)
            copy = pltpu.make_async_remote_copy(
                src_ref=src, dst_ref=dst, send_sem=send_sem.at[level % 2, index], recv_sem=recv_sem.at[level, index],
                device_id=device, device_id_type=MESH)
            result.append((target, source, copy))
        return result

    def send(level, across):
        for target, _, copy in copies(level, across):
            @pl.when(target)
            def _():
                copy.start()

    def receive(level, across):
        for _, source, copy in copies(level, across):
            @pl.when(source)
            def _():
                copy.wait_recv()

    def finish(level):
        for target, _, copy in copies(level, None):
            @pl.when(target)
            def _():
                copy.wait_send()

    def unpack(level, target):
        lv = LEVELS[level]
        rows, width = lv["keep"], lv["width"]
        lane = iota((rows, 128), 1)
        (hi, hi_count, hi_skip), (lo, lo_count, lo_skip) = lv["hi"], lv["lo"]
        is_hi, is_lo = (lane >= hi) & (lane < hi + hi_count), (lane >= lo) & (lane < lo + lo_count)
        for first, count, g, j0 in lv["runs"]:
            for i in range(count):
                e, j = first + i, width * (j0 + i)
                low = pltpu.roll(halo[level][0, g], (lo - lo_skip - j) % 128, 1)
                high = pltpu.roll(halo[level][1, g], (hi - hi_skip - j) % 128, 1)
                if level == 2:
                    place, shift = coarse_place(e)
                    own = ext[level][place, 0:rows, :]
                    own = pltpu.roll(own, 128 - shift, 1) if shift else own
                else:
                    own = 0.0 if level == 0 else ext[level][e, 0:rows, :]
                v = pick(is_hi, high, pick(is_lo, low, own))
                target[e] = pick(lane < 64, v, pltpu.roll(v, 64, 1)) if level == 2 else v

    load.wait()
    pack_faces(0)
    reach = [1 + jnp.minimum(g, 1) + jnp.minimum(n - 1 - g, 1) for g, n in ((gz, nz), (gy, ny), (gx, nx))]
    pl.semaphore_wait(barrier, reach[0] * reach[1] * reach[2] - 1)
    send(0, False)
    send(0, True)

    load_taps.wait()

    def tap_row(level, term):
        return [taps[level, term, k] for k in range(17)]

    def tap_pair(level, second):
        return [jnp.where(second, taps[level, 1, k], taps[level, 0, k]) for k in range(17)]

    def inside(coord, g, n, count):
        return (coord + g * n >= 0) & (coord + g * n < n * count)

    for t in range(2):
        high, low = split(band(x_coords(iota((256, 128), 0), 0) - iota((256, 128), 1), tap_row(0, t)))
        cols = slice(128 * t, 128 * (t + 1))
        x0[0:256, cols], x0[256:512, cols], x0[512:768, cols] = high, high, low
    sq = (128, 128)
    row, col = iota(sq, 0), iota(sq, 1)
    m, c = col - 1, col - 2
    high = pick((m < 66) & inside(m, gx, 64, nx), weight(row - 2 * m), 0.0).astype(BF16)
    xr1[0:128], xr1[128:256] = high, high
    high = pick((row < 67) & (c < 35) & inside(c, gx, 32, nx), weight(row - 1 - 2 * c), 0.0).astype(BF16)
    xr2[0:128], xr2[128:256] = high, high
    m_col, m_row, c_col, c_row = col - 1, row - 1, col - 2, row - 2
    up1 = pick(m_row < 66, weight(col - 2 * m_row), 0.0)
    up2 = pick((c_row < 35) & (m_col < 66) & inside(m_col, gx, 64, nx), weight(m_col - 2 * c_row), 0.0)
    up21 = exact(up2, up1)
    for t in range(2):
        k1 = pick((m_col < 66) & inside(m_col, gx, 64, nx), band(x_coords(row, 1) - m_col, tap_row(1, t)), 0.0)
        high, low = split(exact(k1, up1))
        for first, part in ((0, high), (256, high), (512, low)):
            x1[first + 128 * t : first + 128 * (t + 1)] = part
    k2 = band(x_coords(pick(row < 64, row, row - 64), 2) - c_col, tap_pair(2, row >= 64))
    k2 = pick((c_col < 35) & inside(c_col, gx, 32, nx), k2, 0.0)
    high, low = split(exact(k2, up21))
    x2[0:128], x2[128:256], x2[256:384] = high, high, low

    row, col = iota((32, 128), 0), iota((32, 128), 1)
    m = pick(row < 24, row - 2, row - 24 + 3)
    yr1[...] = pick((m < 19) & inside(m, gy, 16, ny), weight(y_coords(col, 0) - 2 * m), 0.0).astype(BF16)
    for t in range(2):
        y0[64 * t : 64 * t + 32], y0[64 * t + 32 : 64 * t + 64] = split(band(y_coords(col, 0) - row, tap_row(0, t)))
    m_col = col - 1
    yup1 = pick(m_col < 18, weight(row - 2 * m_col), 0.0)
    row, col = iota((24, 128), 0), iota((24, 128), 1)
    c = pick(row < 16, row - 3, row - 16 + 4)
    yr2[...] = pick((c < 12) & inside(c, gy, 8, ny), weight(y_coords(col, 1) - 2 * c), 0.0).astype(BF16)
    row, col = iota(sq, 0), iota(sq, 1)
    m_row, c_col, c_row = row - 1, col - 2, row - 2
    yup2 = pick((m_row < 18) & inside(m_row, gy, 16, ny) & (c_col < 11), weight(m_row - 2 * c_col), 0.0)
    yup21 = exact(yup1, yup2)
    for t in range(2):
        k1 = pick((m_row < 18) & inside(m_row, gy, 16, ny), band(y_coords(col, 1) - m_row, tap_row(1, t)), 0.0)
        y1[64 * t : 64 * t + 32], y1[64 * t + 32 : 64 * t + 64] = split(exact(yup1, k1))
        k2 = pick((c_row < 11) & inside(c_row, gy, 8, ny), band(y_coords(col, 2) - c_row, tap_row(2, t)), 0.0)
        y2[32 * t : 32 * t + 32], y2[64 + 32 * t : 96 + 32 * t] = split(exact(yup21, k2))

    z_low = jnp.where(gz > 0, 1.0, 0.0).astype(F32)
    z_high = jnp.where(gz < nz - 1, 1.0, 0.0).astype(F32)

    def edge(v, low, high):
        n = v.shape[0]
        return jnp.concatenate([v[:low] * z_low, v[low : n - high], v[n - high :] * z_high], axis=0)

    def pieces(v, count):
        return [v[:, 128 * i : 128 * (i + 1)] for i in range(count)]

    receive(0, False)

    def restrict_z(i, _):
        rows = pl.ds(pl.multiple_of(8 * i, 8), 8)
        even, odd = (jnp.concatenate([e0[2 * k + h : 2 * k + h + 1, rows, :] for k in range(24)], axis=0) for h in range(2))
        v = even[2:23] + 0.5625 * (odd[1:22] + odd[2:23]) - 0.0625 * (odd[0:21] + odd[3:24])
        r0[:, rows, :] = edge(v, 2, 3)
        return 0

    lax.fori_loop(0, 6, restrict_z, 0)
    for p in range(0, 21, 7):
        high, low = split(join([r0[p + i] for i in range(7)], 1))
        v = join(pieces(dot(yr1[:, 0:48], high) + dot(yr1[:, 0:48], low), 7), 0)
        v = dot(join(split(v), 1), xr1[...]).reshape(7, 32, 128)
        for i in range(7):
            e1[7 + p + i, 8:32, :] = v[i, 0:24]
            e1[7 + p + i, 40:48, :] = v[i, 24:32]
    send(1, False)
    pack_faces(1)
    send(1, True)
    receive(0, True)
    unpack(0, side)

    def conv_x0(i, _):
        planes = pl.ds(16 * i, 16)
        own_high, own_low = split(e0[planes].reshape(768, 128))
        side_high, side_low = split(side[planes].reshape(768, 128))
        left = join([own_high, side_high, own_low, side_low, own_high, side_high], 1)
        v = dot(left, x0[...])
        for t in range(2):
            f0[t, planes] = v[:, 128 * t : 128 * (t + 1)].reshape(16, 48, 128)
        return 0

    lax.fori_loop(0, 3, conv_x0, 0)

    finish(0)
    receive(1, False)

    def restrict_z1(i, _):
        rows = pl.ds(pl.multiple_of(8 * i, 8), 8)
        even = jnp.concatenate([e1[2 * k : 2 * k + 1, rows, :] for k in range(18)], axis=0)
        odd = jnp.concatenate([e1[2 * k + 1 : 2 * k + 2, rows, :] for k in range(17)], axis=0)
        v = odd[1:16] + 0.5625 * (even[1:16] + even[2:17]) - 0.0625 * (even[0:15] + even[3:18])
        r1[:, rows, :] = edge(v, 3, 4)
        return 0

    lax.fori_loop(0, 5, restrict_z1, 0)
    high, low = split(join([r1[p] for p in range(15)], 1))
    v = dot(yr2[:, 0:40], high) + dot(yr2[:, 0:40], low)
    v = dot(join(split(join(pieces(v, 15), 0)), 1), xr2[...]).reshape(15, 24, 128)
    for g in range(6):
        w = None
        for k in range(3):
            p = 3 * g - 2 + k
            if 0 <= p < 15:
                part = pltpu.roll(v[p], 42 * k, 1) if k else v[p]
                w = part if w is None else w + part
        e2[3 + g, 8:24, :] = w[0:16]
        e2[3 + g, 32:40, :] = w[16:24]
    pack_faces(2)
    send(2, True)
    send(2, False)

    def fine_y(i, _):
        for t in range(2):
            high, low = split(join([f0[t, 6 * i + k] for k in range(6)], 1))
            matrix = y0[64 * t : 64 * t + 64, 0:48]
            both = dot(matrix, high)
            v = pieces(both[0:32] + both[32:64] + dot(matrix[0:32], low), 6)
            for k in range(6):
                s0[t, 6 * i + k] = v[k]
        return 0

    lax.fori_loop(0, 8, fine_y, 0)


    def conv_z(field, row, count):
        total = row[0] * field(0, count)
        for k in range(1, 17):
            total = total + row[k] * field(k, count)
        return total

    def conv_z0(i, _):
        rows = pl.ds(pl.multiple_of(8 * i, 8), 8)
        v = conv_z(lambda k, n: s0[0, k : k + n, rows, :], tap_row(0, 0), 32)
        v = v + conv_z(lambda k, n: s0[1, k : k + n, rows, :], tap_row(0, 1), 32)
        for k in range(32):
            out[k // 2, k % 2, rows, :] = v[k]
        return 0

    lax.fori_loop(0, 4, conv_z0, 0)

    receive(1, True)
    unpack(1, v1)

    def conv_z1(i, _):
        rows = pl.ds(pl.multiple_of(8 * i, 8), 8)
        for t in range(2):
            z1[t, :, rows, :] = edge(conv_z(lambda k, n: v1[k : k + n, rows, :], tap_row(1, t), 19), 1, 2)
        return 0

    lax.fori_loop(0, 5, conv_z1, 0)
    for t in range(2):
        for p, n in ((0, 7), (7, 6), (13, 6)):
            high, low = split(join([z1[t, p + i] for i in range(n)], 1))
            both = dot(y1[64 * t : 64 * t + 64, 0:40], high)
            v = both[0:32] + both[32:64] + dot(y1[64 * t : 64 * t + 32, 0:40], low)
            for i, piece in enumerate(pieces(v, n)):
                q1h[p + i, :, 128 * t : 128 * (t + 1)], q1l[p + i, :, 128 * t : 128 * (t + 1)] = split(piece)
    for p, n in ((0, 7), (7, 6), (13, 6)):
        high, low = (r[p : p + n].reshape(32 * n, 256) for r in (q1h, q1l))
        t1[p : p + n] = dot(join([high, low, high], 1), x1[...]).reshape(n, 32, 128)

    def refine(g, n):
        even = g[1 : n + 1]
        return even, 0.5625 * (even + g[2 : n + 2]) - 0.0625 * (g[0:n] + g[3 : n + 3])

    def add_middle(i, _):
        rows = pl.ds(pl.multiple_of(8 * i, 8), 8)
        for h, v in enumerate(refine(t1[:, rows, :], 16)):
            out[:, h, rows, :] = out[:, h, rows, :] + v
        return 0

    lax.fori_loop(0, 4, add_middle, 0)

    finish(1)
    finish(2)
    receive(2, None)
    unpack(2, v2)

    first_term = iota((8, 128), 1) < 64

    def conv_z2(i, _):
        rows = pl.ds(pl.multiple_of(8 * i, 8), 8)
        row = [v[None] for v in tap_pair(2, jnp.logical_not(first_term))]
        z2[:, rows, :] = edge(conv_z(lambda k, n: v2[k : k + n, rows, :], row, 13), 2, 3)
        return 0

    lax.fori_loop(0, 4, conv_z2, 0)
    lane = iota((32, 128), 1)
    for p, n in ((0, 7), (7, 6)):
        high, low = split(join([z2[p + i] for i in range(n)], 1))
        both, rest = dot(y2[:, 0:32], high), dot(y2[0:64, 0:32], low)
        terms = [pieces(both[32 * t : 32 * t + 32] + both[64 + 32 * t : 96 + 32 * t] + rest[32 * t : 32 * t + 32], n) for t in range(2)]
        high, low = split(join([pick(lane < 64, a, b) for a, b in zip(*terms)], 0))
        t2[p : p + n] = dot(join([high, low, high], 1), x2[...]).reshape(n, 32, 128)

    def add_coarse(i, _):
        rows = pl.ds(pl.multiple_of(8 * i, 8), 8)
        h = t2[:, rows, :]
        even = h[2:11]
        odd = 0.5625 * (h[1:11] + h[2:12]) - 0.0625 * (h[0:10] + h[3:13])
        g = []
        for k in range(9):
            g += [odd[k : k + 1], even[k : k + 1]]
        g = edge(jnp.concatenate(g + [odd[9:10]], axis=0), 1, 2)
        for h, v in enumerate(refine(g, 16)):
            out[:, h, rows, :] = out[:, h, rows, :] + v
        return 0

    lax.fori_loop(0, 4, add_coarse, 0)


def solution(mesh):
    counts = tuple(mesh.shape[a] for a in ("gz", "gy", "gx"))

    def local(charges, kernel_taps):
        vm = pltpu.VMEM
        scratch = [
            vm((48, 48, 128), F32), vm((35, 48, 128), F32), vm((12, 40, 128), F32),
            vm((2, 4, 48, 128), F32), vm((2, 5, 40, 128), F32), vm((2, 4, 32, 128), F32),
            vm((2, 2, 32, 128), F32), vm((2, 4, 32, 128), F32), vm((2, 3, 24, 128), F32),
            vm((48, 48, 128), F32), vm((35, 40, 128), F32), vm((29, 32, 128), F32),
            vm((21, 48, 128), F32), vm((15, 40, 128), F32), vm((2, 48, 48, 128), F32), vm((2, 48, 32, 128), F32),
            vm((2, 19, 40, 128), F32), vm((19, 32, 256), BF16), vm((19, 32, 256), BF16), vm((19, 32, 128), F32),
            vm((13, 32, 128), F32), vm((13, 32, 128), F32),
            vm((768, 256), BF16), vm((256, 128), BF16), vm((768, 128), BF16), vm((256, 128), BF16), vm((384, 128), BF16),
            vm((32, 128), BF16), vm((24, 128), BF16), vm((128, 128), BF16), vm((128, 128), BF16), vm((128, 128), BF16),
            pltpu.SMEM((3, 2, 17), F32),
            pltpu.SemaphoreType.DMA, pltpu.SemaphoreType.DMA, pltpu.SemaphoreType.DMA((2, 26)), pltpu.SemaphoreType.DMA((3, 26)),
        ]
        result = pl.pallas_call(
            functools.partial(kernel, counts),
            out_shape=jax.ShapeDtypeStruct((16, 2, 32, 128), F32),
            in_specs=[pl.BlockSpec(memory_space=pltpu.HBM)] * 2,
            out_specs=pl.BlockSpec(memory_space=pltpu.VMEM),
            scratch_shapes=scratch,
            compiler_params=pltpu.CompilerParams(
                collective_id=0, has_side_effects=True, vmem_limit_bytes=26 * 1024 * 1024),
        )(*(pltpu.with_memory_space_constraint(a, pltpu.HBM) for a in (charges, kernel_taps)))
        return result.reshape(32, 32, 128)

    return jax.shard_map(
        local, mesh=mesh, in_specs=(P("gz", "gy", "gx"), P()), out_specs=P("gz", "gy", "gx"), check_vma=False)
```

```python
import functools
import math

import jax
import jax.numpy as jnp
from jax import lax
from jax.experimental import pallas as pl
from jax.experimental.pallas import tpu as pltpu
from jax.sharding import PartitionSpec as P

F32, BF16 = jnp.float32, jnp.bfloat16
MESH = pl.DeviceIdType.MESH
NOWHERE = -10000

LEVELS = (
    dict(keep=48, own=(8, 32), z={0: (8, 8, 32), 1: (32, 0, 8), -1: (8, 40, 8)},
         y={0: (8, 8, 32), 1: (32, 0, 8), -1: (8, 40, 8)}, tiles=((8, 32),), packrows=32, groups=(0, 16), width=8,
         py={0: (0, 8, 32), 1: (24, 0, 8), -1: (0, 40, 8)}, pg={0: (0, 1, 2), 1: (1, 0, 1), -1: (0, 3, 1)},
         face=(120, 0), hi=(80, 8, 0), lo=(88, 8, 0), runs=((0, 8, 0, 8), (8, 16, 1, 0), (24, 16, 2, 0), (40, 8, 3, 0))),
    dict(keep=40, own=(7, 21), z={0: (7, 7, 21), 1: (16, 0, 7), -1: (12, 28, 7)},
         y={0: (8, 8, 24), 1: (16, 0, 8), -1: (40, 32, 8)}, tiles=((8, 24), (40, 8)), packrows=32, groups=(0, 8, 16, 4), width=16,
         py={0: (0, 8, 24), 1: (8, 0, 8), -1: (24, 32, 8)}, pg={0: (0, 1, 3), 1: (1, 0, 1), -1: (3, 4, 1)},
         face=(51, 0), hi=(80, 16, 0), lo=(96, 16, 0), runs=((0, 7, 0, 1), (7, 8, 1, 0), (15, 8, 2, 0), (23, 5, 3, 0), (28, 7, 4, 1))),
    dict(keep=32, own=(7, 15), z={0: (3, 3, 6), 1: (4, 0, 3), -1: (6, 9, 3)},
         y={0: (8, 8, 16), 1: (8, 0, 8), -1: (32, 24, 8)}, tiles=((8, 16), (32, 8)), packrows=24, groups=(0, 8, 7), width=16,
         py={0: (0, 8, 16), 1: (0, 0, 8), -1: (16, 24, 8)}, pg={0: (0, 1, 2), 1: (0, 0, 1), -1: (2, 3, 1)},
         face=(21, 0), hi=(37, 13, 0), lo=(50, 13, 3), runs=((0, 7, 0, 1), (7, 8, 1, 0), (15, 7, 2, 0), (22, 7, 3, 0))),
)
STEPS = tuple((dz, dy, dx) for dx in (1, -1, 0) for dy in (1, -1, 0) for dz in (1, -1, 0) if (dz, dy, dx) != (0, 0, 0))


def coarse_place(e):
    if e < 7:
        return e // 3, 42 * (e % 3)
    if e < 22:
        return 3 + (e - 5) // 3, 42 * ((e - 5) % 3)
    return 9 + (e - 22) // 3, 42 * ((e - 22) % 3)


def split(x):
    high = x.astype(BF16)
    return high, (x - high.astype(F32)).astype(BF16)


def iota(shape, axis):
    return lax.broadcasted_iota(jnp.int32, shape, axis)


def pick(condition, value, other):
    return jnp.where(condition, value, other)


def dot(a, b):
    return jnp.dot(a, b, preferred_element_type=F32)


def join(parts, axis):
    return parts[0] if len(parts) == 1 else jnp.concatenate(parts, axis=axis)


def exact(a, b):
    return jnp.dot(a, b, preferred_element_type=F32, precision=lax.Precision.HIGHEST)


def weight(d):
    d = jnp.abs(d)
    return pick(d == 0, 1.0, pick(d == 1, 0.5625, pick(d == 3, -0.0625, 0.0))).astype(F32)


def band(diff, row):
    total = jnp.zeros(diff.shape, F32)
    for k in range(17):
        total = pick(diff == k - 8, row[k], total)
    return total


def x_coords(slot, level):
    base, first, high, low, tile = ((128, 0, 128, -8, 128), (67, -1, 63, -14, 0), (37, -2, 30, -10, 0))[level]
    coord = pick(slot < base, slot + first, NOWHERE)
    for (start, count, _), value in ((LEVELS[level]["hi"], high), (LEVELS[level]["lo"], low)):
        k = slot - tile - start
        coord = pick((k >= 0) & (k < count), k + value, coord)
    return coord


def y_coords(row, level):
    if level == 0:
        return row - 8
    if level == 1:
        coord = pick(row < 8, row - 10, pick(row < 29, row - 10, NOWHERE))
        return pick((row >= 32) & (row < 40), row - 32 + 19, coord)
    coord = pick(row < 8, row - 11, pick(row < 23, row - 11, NOWHERE))
    return pick((row >= 24) & (row < 32), row - 24 + 12, coord)


def kernel(counts, q_hbm, taps_hbm, out, *scratch):
    (e0, e1, e2, px0, px1, px2, pk0, pk1, pk2, side, v1, v2, r0, r1, f0, s0, z1, q1h, q1l, t1, z2, t2,
     x0, xr1, x1, xr2, x2, yr1, yr2, y0, y1, y2, taps, local_sem, taps_sem, measure, send_sem, recv_sem) = scratch
    ext, halo, pack = (e0, e1, e2), (px0, px1, px2), (pk0, pk1, pk2)
    nz, ny, nx = counts
    gz, gy, gx = lax.axis_index("gz"), lax.axis_index("gy"), lax.axis_index("gx")

    def neighbour(step, sign):
        dz, dy, dx = (sign * s for s in step)
        z, y, x = gz + dz, gy + dy, gx + dx
        here = None
        for d, v, n in ((dz, z, nz), (dy, y, ny), (dx, x, nx)):
            test = v < n if d > 0 else (v >= 0 if d < 0 else None)
            if test is not None:
                here = test if here is None else here & test
        return here, {"gz": z, "gy": y, "gx": x}

    load = pltpu.make_async_copy(q_hbm, e0.at[pl.ds(8, 32), pl.ds(8, 32), :], local_sem)
    load.start()
    load_taps = pltpu.make_async_copy(taps_hbm, taps, taps_sem)
    load_taps.start()

    barrier = pltpu.get_barrier_semaphore()
    for step in STEPS:
        here, device = neighbour(step, 1)

        @pl.when(here)
        def _():
            pl.semaphore_signal(barrier, inc=1, device_id=device, device_id_type=MESH)

    def places(level, step):
        lv = LEVELS[level]
        dz, dy, dx = step
        if dx == 0:
            z, y = lv["z"][dz], lv["y"][dy]
            src = ext[level].at[pl.ds(z[0], z[2]), pl.ds(y[0], y[2]), :]
            dst = ext[level].at[pl.ds(z[1], z[2]), pl.ds(y[1], y[2]), :]
        else:
            face = 0 if dx == 1 else 1
            z, y = lv["pg"][dz], lv["py"][dy]
            src = pack[level].at[face, pl.ds(z[0], z[2]), pl.ds(y[0], y[2]), :]
            dst = halo[level].at[face, pl.ds(z[1], z[2]), pl.ds(y[1], y[2]), :]
        return src, dst

    for level in range(3):
        for step in STEPS:
            source, _ = neighbour(step, -1)
            _, dst = places(level, step)

            @pl.when(jnp.logical_not(source))
            def _():
                dst[...] = jnp.zeros(dst.shape, F32)

    def pack_faces(level):
        lv, src, width = LEVELS[level], ext[level], LEVELS[level]["width"]
        start, planes = lv["own"]
        lane = iota((lv["packrows"], 128), 1) // width
        for g, offset in enumerate(lv["groups"]):
            faces = [jnp.zeros((lv["packrows"], 128), F32) for _ in range(2)]
            for j in range(min(128 // width, planes - offset)):
                e, shift = start + offset + j, width * j
                if level == 2:
                    e, first = coarse_place(e)
                    shift -= first
                v = join([src[e, r : r + n, :] for r, n in lv["tiles"]], 0)
                for f in range(2):
                    faces[f] = pick(lane == j, pltpu.roll(v, (shift - lv["face"][f]) % 128, 1), faces[f])
            for f in range(2):
                pack[level][f, g] = faces[f]

    def copies(level, across):
        result = []
        for step in STEPS:
            if across is not None and (step[2] != 0) != across:
                continue
            target, device = neighbour(step, 1)
            src, dst = places(level, step)
            copy = pltpu.make_async_remote_copy(
                src_ref=src, dst_ref=dst, send_sem=send_sem.at[level, step[2] % 3], recv_sem=recv_sem.at[level, step[2] % 3],
                device_id=device, device_id_type=MESH)
            result.append((target, copy))
        return result

    def send(level, across):
        for target, copy in copies(level, across):
            @pl.when(target)
            def _():
                copy.start()

    def wait_all(level, semaphores, sign, kinds):
        places_z = (gz == 0, (gz > 0) & (gz < nz - 1), gz == nz - 1)
        places_y = (gy == 0, (gy > 0) & (gy < ny - 1), gy == ny - 1)
        for dx in kinds:
            side = {0: gx >= 0, 1: gx < nx - 1, -1: gx > 0}[sign * dx]
            for z, at_z in enumerate(places_z):
                for y, at_y in enumerate(places_y):
                    units = 0
                    for step in STEPS:
                        if step[2] == dx and 0 <= z + sign * step[0] <= 2 and 0 <= y + sign * step[1] <= 2:
                            shape = places(level, step)[1].shape
                            units += math.prod(shape) // 1024
                    whole = measure.at[pl.ds(0, units)]

                    @pl.when(at_z & at_y & side)
                    def _():
                        pltpu.make_async_copy(whole, whole, semaphores.at[level, dx % 3]).wait()

    def receive(level, across):
        wait_all(level, recv_sem, -1, {None: (0, 1, -1), False: (0,), True: (1, -1)}[across])

    def finish(level):
        wait_all(level, send_sem, 1, (0, 1, -1))

    def unpack(level, target):
        lv = LEVELS[level]
        rows, width = lv["keep"], lv["width"]
        lane = iota((rows, 128), 1)
        (hi, hi_count, hi_skip), (lo, lo_count, lo_skip) = lv["hi"], lv["lo"]
        is_hi, is_lo = (lane >= hi) & (lane < hi + hi_count), (lane >= lo) & (lane < lo + lo_count)
        for first, count, g, j0 in lv["runs"]:
            for i in range(count):
                e, j = first + i, width * (j0 + i)
                low = pltpu.roll(halo[level][0, g], (lo - lo_skip - j) % 128, 1)
                high = pltpu.roll(halo[level][1, g], (hi - hi_skip - j) % 128, 1)
                if level == 2:
                    place, shift = coarse_place(e)
                    own = ext[level][place, 0:rows, :]
                    own = pltpu.roll(own, 128 - shift, 1) if shift else own
                else:
                    own = 0.0 if level == 0 else ext[level][e, 0:rows, :]
                v = pick(is_hi, high, pick(is_lo, low, own))
                target[e] = pick(lane < 64, v, pltpu.roll(v, 64, 1)) if level == 2 else v

    load.wait()
    pack_faces(0)
    reach = [1 + jnp.minimum(g, 1) + jnp.minimum(n - 1 - g, 1) for g, n in ((gz, nz), (gy, ny), (gx, nx))]
    pl.semaphore_wait(barrier, reach[0] * reach[1] * reach[2] - 1)
    send(0, False)
    send(0, True)

    load_taps.wait()

    def tap_row(level, term):
        return [taps[level, term, k] for k in range(17)]

    def tap_pair(level, second):
        return [jnp.where(second, taps[level, 1, k], taps[level, 0, k]) for k in range(17)]

    def inside(coord, g, n, count):
        return (coord + g * n >= 0) & (coord + g * n < n * count)

    for t in range(2):
        high, low = split(band(x_coords(iota((256, 128), 0), 0) - iota((256, 128), 1), tap_row(0, t)))
        cols = slice(128 * t, 128 * (t + 1))
        x0[0:256, cols], x0[256:512, cols], x0[512:768, cols] = high, high, low
    sq = (128, 128)
    row, col = iota(sq, 0), iota(sq, 1)
    m, c = col - 1, col - 2
    high = pick((m < 66) & inside(m, gx, 64, nx), weight(row - 2 * m), 0.0).astype(BF16)
    xr1[0:128], xr1[128:256] = high, high
    high = pick((row < 67) & (c < 35) & inside(c, gx, 32, nx), weight(row - 1 - 2 * c), 0.0).astype(BF16)
    xr2[0:128], xr2[128:256] = high, high
    m_col, m_row, c_col, c_row = col - 1, row - 1, col - 2, row - 2
    up1 = pick(m_row < 66, weight(col - 2 * m_row), 0.0)
    up2 = pick((c_row < 35) & (m_col < 66) & inside(m_col, gx, 64, nx), weight(m_col - 2 * c_row), 0.0)
    up21 = exact(up2, up1)
    for t in range(2):
        k1 = pick((m_col < 66) & inside(m_col, gx, 64, nx), band(x_coords(row, 1) - m_col, tap_row(1, t)), 0.0)
        high, low = split(exact(k1, up1))
        for first, part in ((0, high), (256, high), (512, low)):
            x1[first + 128 * t : first + 128 * (t + 1)] = part
    k2 = band(x_coords(pick(row < 64, row, row - 64), 2) - c_col, tap_pair(2, row >= 64))
    k2 = pick((c_col < 35) & inside(c_col, gx, 32, nx), k2, 0.0)
    high, low = split(exact(k2, up21))
    x2[0:128], x2[128:256], x2[256:384] = high, high, low

    row, col = iota((32, 128), 0), iota((32, 128), 1)
    m = pick(row < 24, row - 2, row - 24 + 3)
    yr1[...] = pick((m < 19) & inside(m, gy, 16, ny), weight(y_coords(col, 0) - 2 * m), 0.0).astype(BF16)
    for t in range(2):
        y0[64 * t : 64 * t + 32], y0[64 * t + 32 : 64 * t + 64] = split(band(y_coords(col, 0) - row, tap_row(0, t)))
    m_col = col - 1
    yup1 = pick(m_col < 18, weight(row - 2 * m_col), 0.0)
    row, col = iota((24, 128), 0), iota((24, 128), 1)
    c = pick(row < 16, row - 3, row - 16 + 4)
    yr2[...] = pick((c < 12) & inside(c, gy, 8, ny), weight(y_coords(col, 1) - 2 * c), 0.0).astype(BF16)
    row, col = iota(sq, 0), iota(sq, 1)
    m_row, c_col, c_row = row - 1, col - 2, row - 2
    yup2 = pick((m_row < 18) & inside(m_row, gy, 16, ny) & (c_col < 11), weight(m_row - 2 * c_col), 0.0)
    yup21 = exact(yup1, yup2)
    for t in range(2):
        k1 = pick((m_row < 18) & inside(m_row, gy, 16, ny), band(y_coords(col, 1) - m_row, tap_row(1, t)), 0.0)
        y1[64 * t : 64 * t + 32], y1[64 * t + 32 : 64 * t + 64] = split(exact(yup1, k1))
        k2 = pick((c_row < 11) & inside(c_row, gy, 8, ny), band(y_coords(col, 2) - c_row, tap_row(2, t)), 0.0)
        y2[32 * t : 32 * t + 32], y2[64 + 32 * t : 96 + 32 * t] = split(exact(yup21, k2))

    z_low = jnp.where(gz > 0, 1.0, 0.0).astype(F32)
    z_high = jnp.where(gz < nz - 1, 1.0, 0.0).astype(F32)

    def edge(v, low, high):
        n = v.shape[0]
        return jnp.concatenate([v[:low] * z_low, v[low : n - high], v[n - high :] * z_high], axis=0)

    def pieces(v, count):
        return [v[:, 128 * i : 128 * (i + 1)] for i in range(count)]

    receive(0, False)

    def restrict_z(i, _):
        rows = pl.ds(pl.multiple_of(8 * i, 8), 8)
        even, odd = (jnp.concatenate([e0[2 * k + h : 2 * k + h + 1, rows, :] for k in range(24)], axis=0) for h in range(2))
        v = even[2:23] + 0.5625 * (odd[1:22] + odd[2:23]) - 0.0625 * (odd[0:21] + odd[3:24])
        r0[:, rows, :] = edge(v, 2, 3)
        return 0

    lax.fori_loop(0, 6, restrict_z, 0)
    for p in range(0, 21, 7):
        high, low = split(join([r0[p + i] for i in range(7)], 1))
        v = join(pieces(dot(yr1[:, 0:48], high) + dot(yr1[:, 0:48], low), 7), 0)
        v = dot(join(split(v), 1), xr1[...]).reshape(7, 32, 128)
        for i in range(7):
            e1[7 + p + i, 8:32, :] = v[i, 0:24]
            e1[7 + p + i, 40:48, :] = v[i, 24:32]
    send(1, False)
    pack_faces(1)
    send(1, True)
    receive(0, True)
    unpack(0, side)

    def conv_x0(i, _):
        planes = pl.ds(16 * i, 16)
        own_high, own_low = split(e0[planes].reshape(768, 128))
        side_high, side_low = split(side[planes].reshape(768, 128))
        left = join([own_high, side_high, own_low, side_low, own_high, side_high], 1)
        v = dot(left, x0[...])
        for t in range(2):
            f0[t, planes] = v[:, 128 * t : 128 * (t + 1)].reshape(16, 48, 128)
        return 0

    lax.fori_loop(0, 3, conv_x0, 0)

    finish(0)
    receive(1, False)

    def restrict_z1(i, _):
        rows = pl.ds(pl.multiple_of(8 * i, 8), 8)
        even = jnp.concatenate([e1[2 * k : 2 * k + 1, rows, :] for k in range(18)], axis=0)
        odd = jnp.concatenate([e1[2 * k + 1 : 2 * k + 2, rows, :] for k in range(17)], axis=0)
        v = odd[1:16] + 0.5625 * (even[1:16] + even[2:17]) - 0.0625 * (even[0:15] + even[3:18])
        r1[:, rows, :] = edge(v, 3, 4)
        return 0

    lax.fori_loop(0, 5, restrict_z1, 0)
    high, low = split(join([r1[p] for p in range(15)], 1))
    v = dot(yr2[:, 0:40], high) + dot(yr2[:, 0:40], low)
    v = dot(join(split(join(pieces(v, 15), 0)), 1), xr2[...]).reshape(15, 24, 128)
    for g in range(6):
        w = None
        for k in range(3):
            p = 3 * g - 2 + k
            if 0 <= p < 15:
                part = pltpu.roll(v[p], 42 * k, 1) if k else v[p]
                w = part if w is None else w + part
        e2[3 + g, 8:24, :] = w[0:16]
        e2[3 + g, 32:40, :] = w[16:24]
    pack_faces(2)
    send(2, True)
    send(2, False)

    def fine_y(i, _):
        for t in range(2):
            high, low = split(join([f0[t, 6 * i + k] for k in range(6)], 1))
            matrix = y0[64 * t : 64 * t + 64, 0:48]
            both = dot(matrix, high)
            v = pieces(both[0:32] + both[32:64] + dot(matrix[0:32], low), 6)
            for k in range(6):
                s0[t, 6 * i + k] = v[k]
        return 0

    lax.fori_loop(0, 8, fine_y, 0)


    def conv_z(field, row, count):
        total = row[0] * field(0, count)
        for k in range(1, 17):
            total = total + row[k] * field(k, count)
        return total

    def conv_z0(i, _):
        rows = pl.ds(pl.multiple_of(8 * i, 8), 8)
        v = conv_z(lambda k, n: s0[0, k : k + n, rows, :], tap_row(0, 0), 32)
        v = v + conv_z(lambda k, n: s0[1, k : k + n, rows, :], tap_row(0, 1), 32)
        for k in range(32):
            out[k // 2, k % 2, rows, :] = v[k]
        return 0

    lax.fori_loop(0, 4, conv_z0, 0)

    receive(1, True)
    unpack(1, v1)

    def conv_z1(i, _):
        rows = pl.ds(pl.multiple_of(8 * i, 8), 8)
        for t in range(2):
            z1[t, :, rows, :] = edge(conv_z(lambda k, n: v1[k : k + n, rows, :], tap_row(1, t), 19), 1, 2)
        return 0

    lax.fori_loop(0, 5, conv_z1, 0)
    for t in range(2):
        for p, n in ((0, 7), (7, 6), (13, 6)):
            high, low = split(join([z1[t, p + i] for i in range(n)], 1))
            both = dot(y1[64 * t : 64 * t + 64, 0:40], high)
            v = both[0:32] + both[32:64] + dot(y1[64 * t : 64 * t + 32, 0:40], low)
            for i, piece in enumerate(pieces(v, n)):
                q1h[p + i, :, 128 * t : 128 * (t + 1)], q1l[p + i, :, 128 * t : 128 * (t + 1)] = split(piece)
    for p, n in ((0, 7), (7, 6), (13, 6)):
        high, low = (r[p : p + n].reshape(32 * n, 256) for r in (q1h, q1l))
        t1[p : p + n] = dot(join([high, low, high], 1), x1[...]).reshape(n, 32, 128)

    def refine(g, n):
        even = g[1 : n + 1]
        return even, 0.5625 * (even + g[2 : n + 2]) - 0.0625 * (g[0:n] + g[3 : n + 3])

    def add_middle(i, _):
        rows = pl.ds(pl.multiple_of(8 * i, 8), 8)
        for h, v in enumerate(refine(t1[:, rows, :], 16)):
            out[:, h, rows, :] = out[:, h, rows, :] + v
        return 0

    lax.fori_loop(0, 4, add_middle, 0)

    finish(1)
    finish(2)
    receive(2, None)
    unpack(2, v2)

    first_term = iota((8, 128), 1) < 64

    def conv_z2(i, _):
        rows = pl.ds(pl.multiple_of(8 * i, 8), 8)
        row = [v[None] for v in tap_pair(2, jnp.logical_not(first_term))]
        z2[:, rows, :] = edge(conv_z(lambda k, n: v2[k : k + n, rows, :], row, 13), 2, 3)
        return 0

    lax.fori_loop(0, 4, conv_z2, 0)
    lane = iota((32, 128), 1)
    for p, n in ((0, 7), (7, 6)):
        high, low = split(join([z2[p + i] for i in range(n)], 1))
        both, rest = dot(y2[:, 0:32], high), dot(y2[0:64, 0:32], low)
        terms = [pieces(both[32 * t : 32 * t + 32] + both[64 + 32 * t : 96 + 32 * t] + rest[32 * t : 32 * t + 32], n) for t in range(2)]
        high, low = split(join([pick(lane < 64, a, b) for a, b in zip(*terms)], 0))
        t2[p : p + n] = dot(join([high, low, high], 1), x2[...]).reshape(n, 32, 128)

    def add_coarse(i, _):
        rows = pl.ds(pl.multiple_of(8 * i, 8), 8)
        h = t2[:, rows, :]
        even = h[2:11]
        odd = 0.5625 * (h[1:11] + h[2:12]) - 0.0625 * (h[0:10] + h[3:13])
        g = []
        for k in range(9):
            g += [odd[k : k + 1], even[k : k + 1]]
        g = edge(jnp.concatenate(g + [odd[9:10]], axis=0), 1, 2)
        for h, v in enumerate(refine(g, 16)):
            out[:, h, rows, :] = out[:, h, rows, :] + v
        return 0

    lax.fori_loop(0, 4, add_coarse, 0)


def solution(mesh):
    counts = tuple(mesh.shape[a] for a in ("gz", "gy", "gx"))

    def local(charges, kernel_taps):
        vm = pltpu.VMEM
        scratch = [
            vm((48, 48, 128), F32), vm((35, 48, 128), F32), vm((12, 40, 128), F32),
            vm((2, 4, 48, 128), F32), vm((2, 5, 40, 128), F32), vm((2, 4, 32, 128), F32),
            vm((2, 2, 32, 128), F32), vm((2, 4, 32, 128), F32), vm((2, 3, 24, 128), F32),
            vm((48, 48, 128), F32), vm((35, 40, 128), F32), vm((29, 32, 128), F32),
            vm((21, 48, 128), F32), vm((15, 40, 128), F32), vm((2, 48, 48, 128), F32), vm((2, 48, 32, 128), F32),
            vm((2, 19, 40, 128), F32), vm((19, 32, 256), BF16), vm((19, 32, 256), BF16), vm((19, 32, 128), F32),
            vm((13, 32, 128), F32), vm((13, 32, 128), F32),
            vm((768, 256), BF16), vm((256, 128), BF16), vm((768, 128), BF16), vm((256, 128), BF16), vm((384, 128), BF16),
            vm((32, 128), BF16), vm((24, 128), BF16), vm((128, 128), BF16), vm((128, 128), BF16), vm((128, 128), BF16),
            pltpu.SMEM((3, 2, 17), F32),
            pltpu.SemaphoreType.DMA, pltpu.SemaphoreType.DMA, vm((160, 8, 128), F32), pltpu.SemaphoreType.DMA((3, 3)), pltpu.SemaphoreType.DMA((3, 3)),
        ]
        result = pl.pallas_call(
            functools.partial(kernel, counts),
            out_shape=jax.ShapeDtypeStruct((16, 2, 32, 128), F32),
            in_specs=[pl.BlockSpec(memory_space=pltpu.HBM)] * 2,
            out_specs=pl.BlockSpec(memory_space=pltpu.VMEM),
            scratch_shapes=scratch,
            compiler_params=pltpu.CompilerParams(
                collective_id=0, has_side_effects=True, vmem_limit_bytes=26 * 1024 * 1024),
        )(*(pltpu.with_memory_space_constraint(a, pltpu.HBM) for a in (charges, kernel_taps)))
        return result.reshape(32, 32, 128)

    return jax.shard_map(
        local, mesh=mesh, in_specs=(P("gz", "gy", "gx"), P()), out_specs=P("gz", "gy", "gx"), check_vma=False)
```

```python
import functools
import math

import jax
import jax.numpy as jnp
from jax import lax
from jax.experimental import pallas as pl
from jax.experimental.pallas import tpu as pltpu
from jax.sharding import PartitionSpec as P

F32, BF16 = jnp.float32, jnp.bfloat16
MESH = pl.DeviceIdType.MESH
NOWHERE = -10000

LEVELS = (
    dict(keep=48, own=(8, 32), z={0: (8, 8, 32), 1: (32, 0, 8), -1: (8, 40, 8)},
         y={0: (8, 8, 32), 1: (32, 0, 8), -1: (8, 40, 8)}, tiles=((8, 32),), packrows=32, groups=(0, 16), width=8,
         py={0: (0, 8, 32), 1: (24, 0, 8), -1: (0, 40, 8)}, pg={0: (0, 1, 2), 1: (1, 0, 1), -1: (0, 3, 1)},
         face=(120, 0), hi=(80, 8, 0), lo=(88, 8, 0), runs=((0, 8, 0, 8), (8, 16, 1, 0), (24, 16, 2, 0), (40, 8, 3, 0))),
    dict(keep=40, own=(7, 21), z={0: (7, 7, 21), 1: (16, 0, 7), -1: (12, 28, 7)},
         y={0: (8, 8, 24), 1: (16, 0, 8), -1: (40, 32, 8)}, tiles=((8, 24), (40, 8)), packrows=32, groups=(0, 8, 16, 4), width=16,
         py={0: (0, 8, 24), 1: (8, 0, 8), -1: (24, 32, 8)}, pg={0: (0, 1, 3), 1: (1, 0, 1), -1: (3, 4, 1)},
         face=(51, 0), hi=(80, 16, 0), lo=(96, 16, 0), runs=((0, 7, 0, 1), (7, 8, 1, 0), (15, 8, 2, 0), (23, 5, 3, 0), (28, 7, 4, 1))),
    dict(keep=32, own=(7, 15), z={0: (3, 3, 6), 1: (4, 0, 3), -1: (6, 9, 3)},
         y={0: (8, 8, 16), 1: (8, 0, 8), -1: (32, 24, 8)}, tiles=((8, 16), (32, 8)), packrows=24, groups=(0, 8, 7), width=16,
         py={0: (0, 8, 16), 1: (0, 0, 8), -1: (16, 24, 8)}, pg={0: (0, 1, 2), 1: (0, 0, 1), -1: (2, 3, 1)},
         face=(21, 0), hi=(50, 13, 0), lo=(37, 13, 3), runs=((0, 7, 0, 1), (7, 8, 1, 0), (15, 7, 2, 0), (22, 7, 3, 0))),
)
STEPS = tuple((dz, dy, dx) for dx in (1, -1, 0) for dy in (1, -1, 0) for dz in (1, -1, 0) if (dz, dy, dx) != (0, 0, 0))


def coarse_place(e):
    if e < 7:
        return e // 3, 42 * (e % 3)
    if e < 22:
        return 3 + (e - 5) // 3, 42 * ((e - 5) % 3)
    return 9 + (e - 22) // 3, 42 * ((e - 22) % 3)


def split(x):
    high = x.astype(BF16)
    return high, (x - high.astype(F32)).astype(BF16)


def iota(shape, axis):
    return lax.broadcasted_iota(jnp.int32, shape, axis)


def pick(condition, value, other):
    return jnp.where(condition, value, other)


def dot(a, b):
    return jnp.dot(a, b, preferred_element_type=F32)


def join(parts, axis):
    return parts[0] if len(parts) == 1 else jnp.concatenate(parts, axis=axis)


def exact(a, b):
    return jnp.dot(a, b, preferred_element_type=F32, precision=lax.Precision.HIGHEST)


def weight(d):
    d = jnp.abs(d)
    return pick(d == 0, 1.0, pick(d == 1, 0.5625, pick(d == 3, -0.0625, 0.0))).astype(F32)


def band(diff, row):
    total = jnp.zeros(diff.shape, F32)
    for k in range(17):
        total = pick(diff == k - 8, row[k], total)
    return total


def x_coords(slot, level):
    base, first, high, low, tile = ((128, 0, 128, -8, 128), (67, -1, 63, -14, 0), (37, -2, 30, -10, 0))[level]
    coord = pick(slot < base, slot + first, NOWHERE)
    for (start, count, _), value in ((LEVELS[level]["hi"], high), (LEVELS[level]["lo"], low)):
        k = slot - tile - start
        coord = pick((k >= 0) & (k < count), k + value, coord)
    return coord


def y_coords(row, level):
    if level == 0:
        return row - 8
    if level == 1:
        coord = pick(row < 8, row - 10, pick(row < 29, row - 10, NOWHERE))
        return pick((row >= 32) & (row < 40), row - 32 + 19, coord)
    coord = pick(row < 8, row - 11, pick(row < 23, row - 11, NOWHERE))
    return pick((row >= 24) & (row < 32), row - 24 + 12, coord)


def kernel(counts, q_hbm, taps_hbm, out, *scratch):
    (e0, e1, e2, px0, px1, px2, pk0, pk1, pk2, side, v1, v2, r0, r1, f0, s0, z1, q1h, q1l, t1, z2, t2,
     x0, xr1, x1, xr2, x2, yr1, yr2, y0, y1, y2, taps, local_sem, taps_sem, measure, send_sem, recv_sem) = scratch
    ext, halo, pack = (e0, e1, e2), (px0, px1, px2), (pk0, pk1, pk2)
    nz, ny, nx = counts
    gz, gy, gx = lax.axis_index("gz"), lax.axis_index("gy"), lax.axis_index("gx")

    def neighbour(step, sign):
        dz, dy, dx = (sign * s for s in step)
        z, y, x = gz + dz, gy + dy, gx + dx
        here = None
        for d, v, n in ((dz, z, nz), (dy, y, ny), (dx, x, nx)):
            test = v < n if d > 0 else (v >= 0 if d < 0 else None)
            if test is not None:
                here = test if here is None else here & test
        return here, {"gz": z, "gy": y, "gx": x}

    load = pltpu.make_async_copy(q_hbm, e0.at[pl.ds(8, 32), pl.ds(8, 32), :], local_sem)
    load.start()
    load_taps = pltpu.make_async_copy(taps_hbm, taps, taps_sem)
    load_taps.start()

    barrier = pltpu.get_barrier_semaphore()
    for step in STEPS:
        here, device = neighbour(step, 1)

        @pl.when(here)
        def _():
            pl.semaphore_signal(barrier, inc=1, device_id=device, device_id_type=MESH)

    def places(level, step):
        lv = LEVELS[level]
        dz, dy, dx = step
        if dx == 0:
            z, y = lv["z"][dz], lv["y"][dy]
            src = ext[level].at[pl.ds(z[0], z[2]), pl.ds(y[0], y[2]), :]
            dst = ext[level].at[pl.ds(z[1], z[2]), pl.ds(y[1], y[2]), :]
        else:
            face = 0 if dx == 1 else 1
            z, y = lv["pg"][dz], lv["py"][dy]
            src = pack[level].at[face, pl.ds(z[0], z[2]), pl.ds(y[0], y[2]), :]
            dst = halo[level].at[face, pl.ds(z[1], z[2]), pl.ds(y[1], y[2]), :]
        return src, dst

    for level in range(3):
        for step in STEPS:
            source, _ = neighbour(step, -1)
            _, dst = places(level, step)

            @pl.when(jnp.logical_not(source))
            def _():
                dst[...] = jnp.zeros(dst.shape, F32)

    def pack_faces(level):
        lv, src, width = LEVELS[level], ext[level], LEVELS[level]["width"]
        start, planes = lv["own"]
        lane = iota((lv["packrows"], 128), 1) // width
        for g, offset in enumerate(lv["groups"]):
            faces = [jnp.zeros((lv["packrows"], 128), F32) for _ in range(2)]
            for j in range(min(128 // width, planes - offset)):
                e, shift = start + offset + j, width * j
                if level == 2:
                    e, first = coarse_place(e)
                    shift -= first
                v = join([src[e, r : r + n, :] for r, n in lv["tiles"]], 0)
                for f in range(2):
                    faces[f] = pick(lane == j, pltpu.roll(v, (shift - lv["face"][f]) % 128, 1), faces[f])
            for f in range(2):
                pack[level][f, g] = faces[f]

    def copies(level, across):
        result = []
        for step in STEPS:
            if across is not None and (step[2] != 0) != across:
                continue
            target, device = neighbour(step, 1)
            src, dst = places(level, step)
            copy = pltpu.make_async_remote_copy(
                src_ref=src, dst_ref=dst, send_sem=send_sem.at[level, step[2] % 3], recv_sem=recv_sem.at[level, step[2] % 3],
                device_id=device, device_id_type=MESH)
            result.append((target, copy))
        return result

    def send(level, across):
        for target, copy in copies(level, across):
            @pl.when(target)
            def _():
                copy.start()

    def wait_all(level, semaphores, sign, kinds):
        places_z = (gz == 0, (gz > 0) & (gz < nz - 1), gz == nz - 1)
        places_y = (gy == 0, (gy > 0) & (gy < ny - 1), gy == ny - 1)
        for dx in kinds:
            side = {0: gx >= 0, 1: gx < nx - 1, -1: gx > 0}[sign * dx]
            for z, at_z in enumerate(places_z):
                for y, at_y in enumerate(places_y):
                    units = 0
                    for step in STEPS:
                        if step[2] == dx and 0 <= z + sign * step[0] <= 2 and 0 <= y + sign * step[1] <= 2:
                            shape = places(level, step)[1].shape
                            units += math.prod(shape) // 1024
                    whole = measure.at[pl.ds(0, units)]

                    @pl.when(at_z & at_y & side)
                    def _():
                        pltpu.make_async_copy(whole, whole, semaphores.at[level, dx % 3]).wait()

    def receive(level, across):
        wait_all(level, recv_sem, -1, {None: (0, 1, -1), False: (0,), True: (1, -1)}[across])

    def finish(level):
        wait_all(level, send_sem, 1, (0, 1, -1))

    def unpack_own(target):
        lane = iota((32, 128), 1)
        for first, count, _, _ in LEVELS[2]["runs"]:
            for e in range(first, first + count):
                place, shift = coarse_place(e)
                v = e2[place, 0:32, :]
                v = pltpu.roll(v, 128 - shift, 1) if shift else v
                target[e] = pick(lane < 64, v, pltpu.roll(v, 64, 1))

    def unpack(level, target):
        lv = LEVELS[level]
        rows, width = lv["keep"], lv["width"]
        lane = iota((rows, 128), 1)
        start = 34 if level == 2 else lv["hi"][0]
        here = lane % 64 if level == 2 else lane
        used = (here >= 37) & (here < 63) if level == 2 else (lane >= start) & (lane < start + 2 * width)
        even = (lane // width) % 2 == 0
        for first, count, g, j0 in lv["runs"]:
            leading, trailing = (halo[level][0, g], halo[level][1, g]) if level == 2 else (halo[level][1, g], halo[level][0, g])
            trailing = pltpu.roll(trailing, width, 1)
            pair = (pick(even, leading, trailing), pick(even, trailing, leading))
            places = range(8) if level == 2 else range(j0, j0 + count)
            moved = {j: pltpu.roll(pair[j % 2], (start - width * j) % 128, 1) for j in places}
            for i in range(count):
                e, j = first + i, j0 + i
                if level == 2:
                    target[e] = pick(used, pick(lane < 64, moved[j], moved[(j + 4) % 8]), target[e])
                else:
                    target[e] = pick(used, moved[j], 0.0 if level == 0 else ext[level][e, 0:rows, :])

    load.wait()
    pack_faces(0)
    reach = [1 + jnp.minimum(g, 1) + jnp.minimum(n - 1 - g, 1) for g, n in ((gz, nz), (gy, ny), (gx, nx))]
    pl.semaphore_wait(barrier, reach[0] * reach[1] * reach[2] - 1)
    send(0, False)
    send(0, True)

    load_taps.wait()

    def tap_row(level, term):
        return [taps[level, term, k] for k in range(17)]

    def tap_pair(level, second):
        return [jnp.where(second, taps[level, 1, k], taps[level, 0, k]) for k in range(17)]

    def inside(coord, g, n, count):
        return (coord + g * n >= 0) & (coord + g * n < n * count)

    for t in range(2):
        high, low = split(band(x_coords(iota((256, 128), 0), 0) - iota((256, 128), 1), tap_row(0, t)))
        cols = slice(128 * t, 128 * (t + 1))
        x0[0:256, cols], x0[256:512, cols], x0[512:768, cols] = high, high, low
    sq = (128, 128)
    row, col = iota(sq, 0), iota(sq, 1)
    m, c = col - 1, col - 2
    high = pick((m < 66) & inside(m, gx, 64, nx), weight(row - 2 * m), 0.0).astype(BF16)
    xr1[0:128], xr1[128:256] = high, high
    high = pick((row < 67) & (c < 35) & inside(c, gx, 32, nx), weight(row - 1 - 2 * c), 0.0).astype(BF16)
    xr2[0:128], xr2[128:256] = high, high
    m_col, m_row, c_col, c_row = col - 1, row - 1, col - 2, row - 2
    up1 = pick(m_row < 66, weight(col - 2 * m_row), 0.0)
    up2 = pick((c_row < 35) & (m_col < 66) & inside(m_col, gx, 64, nx), weight(m_col - 2 * c_row), 0.0)
    up21 = exact(up2, up1)
    for t in range(2):
        k1 = pick((m_col < 66) & inside(m_col, gx, 64, nx), band(x_coords(row, 1) - m_col, tap_row(1, t)), 0.0)
        high, low = split(exact(k1, up1))
        for first, part in ((0, high), (256, high), (512, low)):
            x1[first + 128 * t : first + 128 * (t + 1)] = part
    k2 = band(x_coords(pick(row < 64, row, row - 64), 2) - c_col, tap_pair(2, row >= 64))
    k2 = pick((c_col < 35) & inside(c_col, gx, 32, nx), k2, 0.0)
    high, low = split(exact(k2, up21))
    x2[0:128], x2[128:256], x2[256:384] = high, high, low

    row, col = iota((32, 128), 0), iota((32, 128), 1)
    m = pick(row < 24, row - 2, row - 24 + 3)
    yr1[...] = pick((m < 19) & inside(m, gy, 16, ny), weight(y_coords(col, 0) - 2 * m), 0.0).astype(BF16)
    for t in range(2):
        y0[64 * t : 64 * t + 32], y0[64 * t + 32 : 64 * t + 64] = split(band(y_coords(col, 0) - row, tap_row(0, t)))
    m_col = col - 1
    yup1 = pick(m_col < 18, weight(row - 2 * m_col), 0.0)
    row, col = iota((24, 128), 0), iota((24, 128), 1)
    c = pick(row < 16, row - 3, row - 16 + 4)
    yr2[...] = pick((c < 12) & inside(c, gy, 8, ny), weight(y_coords(col, 1) - 2 * c), 0.0).astype(BF16)
    row, col = iota(sq, 0), iota(sq, 1)
    m_row, c_col, c_row = row - 1, col - 2, row - 2
    yup2 = pick((m_row < 18) & inside(m_row, gy, 16, ny) & (c_col < 11), weight(m_row - 2 * c_col), 0.0)
    yup21 = exact(yup1, yup2)
    for t in range(2):
        k1 = pick((m_row < 18) & inside(m_row, gy, 16, ny), band(y_coords(col, 1) - m_row, tap_row(1, t)), 0.0)
        y1[64 * t : 64 * t + 32], y1[64 * t + 32 : 64 * t + 64] = split(exact(yup1, k1))
        k2 = pick((c_row < 11) & inside(c_row, gy, 8, ny), band(y_coords(col, 2) - c_row, tap_row(2, t)), 0.0)
        y2[32 * t : 32 * t + 32], y2[64 + 32 * t : 96 + 32 * t] = split(exact(yup21, k2))

    z_low = jnp.where(gz > 0, 1.0, 0.0).astype(F32)
    z_high = jnp.where(gz < nz - 1, 1.0, 0.0).astype(F32)

    def edge(v, low, high):
        n = v.shape[0]
        return jnp.concatenate([v[:low] * z_low, v[low : n - high], v[n - high :] * z_high], axis=0)

    def pieces(v, count):
        return [v[:, 128 * i : 128 * (i + 1)] for i in range(count)]

    receive(0, False)

    def restrict_z(i, _):
        rows = pl.ds(pl.multiple_of(8 * i, 8), 8)
        even, odd = (jnp.concatenate([e0[2 * k + h : 2 * k + h + 1, rows, :] for k in range(24)], axis=0) for h in range(2))
        v = even[2:23] + 0.5625 * (odd[1:22] + odd[2:23]) - 0.0625 * (odd[0:21] + odd[3:24])
        r0[:, rows, :] = edge(v, 2, 3)
        return 0

    lax.fori_loop(0, 6, restrict_z, 0)
    for p in range(0, 21, 7):
        high, low = split(join([r0[p + i] for i in range(7)], 1))
        v = join(pieces(dot(yr1[:, 0:48], high) + dot(yr1[:, 0:48], low), 7), 0)
        v = dot(join(split(v), 1), xr1[...]).reshape(7, 32, 128)
        for i in range(7):
            e1[7 + p + i, 8:32, :] = v[i, 0:24]
            e1[7 + p + i, 40:48, :] = v[i, 24:32]
    send(1, False)
    pack_faces(1)
    send(1, True)
    receive(0, True)
    unpack(0, side)

    def conv_x0(i, _):
        planes = pl.ds(16 * i, 16)
        own_high, own_low = split(e0[planes].reshape(768, 128))
        side_high, side_low = split(side[planes].reshape(768, 128))
        left = join([own_high, side_high, own_low, side_low, own_high, side_high], 1)
        v = dot(left, x0[...])
        for t in range(2):
            f0[t, planes] = v[:, 128 * t : 128 * (t + 1)].reshape(16, 48, 128)
        return 0

    lax.fori_loop(0, 3, conv_x0, 0)

    finish(0)
    receive(1, False)

    def restrict_z1(i, _):
        rows = pl.ds(pl.multiple_of(8 * i, 8), 8)
        even = jnp.concatenate([e1[2 * k : 2 * k + 1, rows, :] for k in range(18)], axis=0)
        odd = jnp.concatenate([e1[2 * k + 1 : 2 * k + 2, rows, :] for k in range(17)], axis=0)
        v = odd[1:16] + 0.5625 * (even[1:16] + even[2:17]) - 0.0625 * (even[0:15] + even[3:18])
        r1[:, rows, :] = edge(v, 3, 4)
        return 0

    lax.fori_loop(0, 5, restrict_z1, 0)
    high, low = split(join([r1[p] for p in range(15)], 1))
    v = dot(yr2[:, 0:40], high) + dot(yr2[:, 0:40], low)
    v = dot(join(split(join(pieces(v, 15), 0)), 1), xr2[...]).reshape(15, 24, 128)
    for g in range(6):
        w = None
        for k in range(3):
            p = 3 * g - 2 + k
            if 0 <= p < 15:
                part = pltpu.roll(v[p], 42 * k, 1) if k else v[p]
                w = part if w is None else w + part
        e2[3 + g, 8:24, :] = w[0:16]
        e2[3 + g, 32:40, :] = w[16:24]
    pack_faces(2)
    send(2, True)
    send(2, False)

    def fine_y(i, _):
        for t in range(2):
            high, low = split(join([f0[t, 6 * i + k] for k in range(6)], 1))
            matrix = y0[64 * t : 64 * t + 64, 0:48]
            both = dot(matrix, high)
            v = pieces(both[0:32] + both[32:64] + dot(matrix[0:32], low), 6)
            for k in range(6):
                s0[t, 6 * i + k] = v[k]
        return 0

    lax.fori_loop(0, 8, fine_y, 0)


    def conv_z(field, row, count):
        total = row[0] * field(0, count)
        for k in range(1, 17):
            total = total + row[k] * field(k, count)
        return total

    def conv_z0(i, _):
        rows = pl.ds(pl.multiple_of(8 * i, 8), 8)
        v = conv_z(lambda k, n: s0[0, k : k + n, rows, :], tap_row(0, 0), 32)
        v = v + conv_z(lambda k, n: s0[1, k : k + n, rows, :], tap_row(0, 1), 32)
        for k in range(32):
            out[k // 2, k % 2, rows, :] = v[k]
        return 0

    lax.fori_loop(0, 4, conv_z0, 0)

    receive(1, True)
    unpack(1, v1)

    def conv_z1(i, _):
        rows = pl.ds(pl.multiple_of(8 * i, 8), 8)
        for t in range(2):
            z1[t, :, rows, :] = edge(conv_z(lambda k, n: v1[k : k + n, rows, :], tap_row(1, t), 19), 1, 2)
        return 0

    lax.fori_loop(0, 5, conv_z1, 0)
    for t in range(2):
        for p, n in ((0, 7), (7, 6), (13, 6)):
            high, low = split(join([z1[t, p + i] for i in range(n)], 1))
            both = dot(y1[64 * t : 64 * t + 64, 0:40], high)
            v = both[0:32] + both[32:64] + dot(y1[64 * t : 64 * t + 32, 0:40], low)
            for i, piece in enumerate(pieces(v, n)):
                q1h[p + i, :, 128 * t : 128 * (t + 1)], q1l[p + i, :, 128 * t : 128 * (t + 1)] = split(piece)
    for p, n in ((0, 7), (7, 6), (13, 6)):
        high, low = (r[p : p + n].reshape(32 * n, 256) for r in (q1h, q1l))
        t1[p : p + n] = dot(join([high, low, high], 1), x1[...]).reshape(n, 32, 128)

    def refine(g, n):
        even = g[1 : n + 1]
        return even, 0.5625 * (even + g[2 : n + 2]) - 0.0625 * (g[0:n] + g[3 : n + 3])

    def add_middle(i, _):
        rows = pl.ds(pl.multiple_of(8 * i, 8), 8)
        for h, v in enumerate(refine(t1[:, rows, :], 16)):
            out[:, h, rows, :] = out[:, h, rows, :] + v
        return 0

    lax.fori_loop(0, 4, add_middle, 0)

    finish(1)
    finish(2)
    receive(2, False)
    unpack_own(v2)
    receive(2, True)
    unpack(2, v2)

    first_term = iota((8, 128), 1) < 64

    def conv_z2(i, _):
        rows = pl.ds(pl.multiple_of(8 * i, 8), 8)
        row = [v[None] for v in tap_pair(2, jnp.logical_not(first_term))]
        z2[:, rows, :] = edge(conv_z(lambda k, n: v2[k : k + n, rows, :], row, 13), 2, 3)
        return 0

    lax.fori_loop(0, 4, conv_z2, 0)
    lane = iota((32, 128), 1)
    for p, n in ((0, 7), (7, 6)):
        high, low = split(join([z2[p + i] for i in range(n)], 1))
        both, rest = dot(y2[:, 0:32], high), dot(y2[0:64, 0:32], low)
        terms = [pieces(both[32 * t : 32 * t + 32] + both[64 + 32 * t : 96 + 32 * t] + rest[32 * t : 32 * t + 32], n) for t in range(2)]
        high, low = split(join([pick(lane < 64, a, b) for a, b in zip(*terms)], 0))
        t2[p : p + n] = dot(join([high, low, high], 1), x2[...]).reshape(n, 32, 128)

    def add_coarse(i, _):
        rows = pl.ds(pl.multiple_of(8 * i, 8), 8)
        h = t2[:, rows, :]
        even = h[2:11]
        odd = 0.5625 * (h[1:11] + h[2:12]) - 0.0625 * (h[0:10] + h[3:13])
        g = []
        for k in range(9):
            g += [odd[k : k + 1], even[k : k + 1]]
        g = edge(jnp.concatenate(g + [odd[9:10]], axis=0), 1, 2)
        for h, v in enumerate(refine(g, 16)):
            out[:, h, rows, :] = out[:, h, rows, :] + v
        return 0

    lax.fori_loop(0, 4, add_coarse, 0)


def solution(mesh):
    counts = tuple(mesh.shape[a] for a in ("gz", "gy", "gx"))

    def local(charges, kernel_taps):
        vm = pltpu.VMEM
        scratch = [
            vm((48, 48, 128), F32), vm((35, 48, 128), F32), vm((12, 40, 128), F32),
            vm((2, 4, 48, 128), F32), vm((2, 5, 40, 128), F32), vm((2, 4, 32, 128), F32),
            vm((2, 2, 32, 128), F32), vm((2, 4, 32, 128), F32), vm((2, 3, 24, 128), F32),
            vm((48, 48, 128), F32), vm((35, 40, 128), F32), vm((29, 32, 128), F32),
            vm((21, 48, 128), F32), vm((15, 40, 128), F32), vm((2, 48, 48, 128), F32), vm((2, 48, 32, 128), F32),
            vm((2, 19, 40, 128), F32), vm((19, 32, 256), BF16), vm((19, 32, 256), BF16), vm((19, 32, 128), F32),
            vm((13, 32, 128), F32), vm((13, 32, 128), F32),
            vm((768, 256), BF16), vm((256, 128), BF16), vm((768, 128), BF16), vm((256, 128), BF16), vm((384, 128), BF16),
            vm((32, 128), BF16), vm((24, 128), BF16), vm((128, 128), BF16), vm((128, 128), BF16), vm((128, 128), BF16),
            pltpu.SMEM((3, 2, 17), F32),
            pltpu.SemaphoreType.DMA, pltpu.SemaphoreType.DMA, vm((160, 8, 128), F32), pltpu.SemaphoreType.DMA((3, 3)), pltpu.SemaphoreType.DMA((3, 3)),
        ]
        result = pl.pallas_call(
            functools.partial(kernel, counts),
            out_shape=jax.ShapeDtypeStruct((16, 2, 32, 128), F32),
            in_specs=[pl.BlockSpec(memory_space=pltpu.HBM)] * 2,
            out_specs=pl.BlockSpec(memory_space=pltpu.VMEM),
            scratch_shapes=scratch,
            compiler_params=pltpu.CompilerParams(
                collective_id=0, has_side_effects=True, vmem_limit_bytes=26 * 1024 * 1024),
        )(*(pltpu.with_memory_space_constraint(a, pltpu.HBM) for a in (charges, kernel_taps)))
        return result.reshape(32, 32, 128)

    return jax.shard_map(
        local, mesh=mesh, in_specs=(P("gz", "gy", "gx"), P()), out_specs=P("gz", "gy", "gx"), check_vma=False)
```

```python
import functools
import math

import jax
import jax.numpy as jnp
from jax import lax
from jax.experimental import pallas as pl
from jax.experimental.pallas import tpu as pltpu
from jax.sharding import PartitionSpec as P

F32, BF16 = jnp.float32, jnp.bfloat16
MESH = pl.DeviceIdType.MESH
NOWHERE = -10000

LEVELS = (
    dict(keep=48, own=(8, 32), z={0: (8, 8, 32), 1: (32, 0, 8), -1: (8, 40, 8)},
         y={0: (8, 8, 32), 1: (32, 0, 8), -1: (8, 40, 8)}, tiles=((8, 32),), packrows=32, groups=(0, 16), width=8,
         py={0: (0, 8, 32), 1: (24, 0, 8), -1: (0, 40, 8)}, pg={0: (0, 1, 2), 1: (1, 0, 1), -1: (0, 3, 1)},
         face=(120, 0), hi=(80, 8, 0), lo=(88, 8, 0), runs=((0, 8, 0, 8), (8, 16, 1, 0), (24, 16, 2, 0), (40, 8, 3, 0))),
    dict(keep=40, own=(7, 21), z={0: (7, 7, 21), 1: (16, 0, 7), -1: (12, 28, 7)},
         y={0: (8, 8, 24), 1: (16, 0, 8), -1: (40, 32, 8)}, tiles=((8, 24), (40, 8)), packrows=32, groups=(0, 8, 16, 4), width=16,
         py={0: (0, 8, 24), 1: (8, 0, 8), -1: (24, 32, 8)}, pg={0: (0, 1, 3), 1: (1, 0, 1), -1: (3, 4, 1)},
         face=(51, 0), hi=(80, 16, 0), lo=(96, 16, 0), runs=((0, 7, 0, 1), (7, 8, 1, 0), (15, 8, 2, 0), (23, 5, 3, 0), (28, 7, 4, 1))),
    dict(keep=32, own=(7, 15), z={0: (3, 3, 6), 1: (4, 0, 3), -1: (6, 9, 3)},
         y={0: (8, 8, 16), 1: (8, 0, 8), -1: (32, 24, 8)}, tiles=((8, 16), (32, 8)), packrows=24, groups=(0, 8, 7), width=16,
         py={0: (0, 8, 16), 1: (0, 0, 8), -1: (16, 24, 8)}, pg={0: (0, 1, 2), 1: (0, 0, 1), -1: (2, 3, 1)},
         face=(21, 0), hi=(50, 13, 0), lo=(37, 13, 3), runs=((0, 7, 0, 1), (7, 8, 1, 0), (15, 7, 2, 0), (22, 7, 3, 0))),
)
STEPS = tuple((dz, dy, dx) for dx in (1, -1, 0) for dy in (1, -1, 0) for dz in (1, -1, 0) if (dz, dy, dx) != (0, 0, 0))


def coarse_place(e):
    if e < 7:
        return e // 3, 42 * (e % 3)
    if e < 22:
        return 3 + (e - 5) // 3, 42 * ((e - 5) % 3)
    return 9 + (e - 22) // 3, 42 * ((e - 22) % 3)


def split(x):
    high = x.astype(BF16)
    return high, (x - high.astype(F32)).astype(BF16)


def iota(shape, axis):
    return lax.broadcasted_iota(jnp.int32, shape, axis)


def pick(condition, value, other):
    return jnp.where(condition, value, other)


def dot(a, b):
    return jnp.dot(a, b, preferred_element_type=F32)


def join(parts, axis):
    return parts[0] if len(parts) == 1 else jnp.concatenate(parts, axis=axis)


def exact(a, b):
    return jnp.dot(a, b, preferred_element_type=F32, precision=lax.Precision.HIGHEST)


def weight(d):
    d = jnp.abs(d)
    return pick(d == 0, 1.0, pick(d == 1, 0.5625, pick(d == 3, -0.0625, 0.0))).astype(F32)


def band(diff, row):
    total = jnp.zeros(diff.shape, F32)
    for k in range(17):
        total = pick(diff == k - 8, row[k], total)
    return total


def x_coords(slot, level):
    base, first, high, low, tile = ((128, 0, 128, -8, 128), (67, -1, 63, -14, 0), (37, -2, 30, -10, 0))[level]
    coord = pick(slot < base, slot + first, NOWHERE)
    for (start, count, _), value in ((LEVELS[level]["hi"], high), (LEVELS[level]["lo"], low)):
        k = slot - tile - start
        coord = pick((k >= 0) & (k < count), k + value, coord)
    return coord


def y_coords(row, level):
    if level == 0:
        return row - 8
    if level == 1:
        coord = pick(row < 8, row - 10, pick(row < 29, row - 10, NOWHERE))
        return pick((row >= 32) & (row < 40), row - 32 + 19, coord)
    coord = pick(row < 8, row - 11, pick(row < 23, row - 11, NOWHERE))
    return pick((row >= 24) & (row < 32), row - 24 + 12, coord)


def kernel(counts, q_hbm, taps_hbm, out, *scratch):
    (e0, e1, e2, px0, px1, px2, pk0, pk1, pk2, side, v1, v2, r0, r1, f0, s0, z1, q1h, q1l, t1, z2, t2,
     x0, xr1, x1, xr2, x2, yr1, yr2, y0, y1, y2, taps, local_sem, taps_sem, measure, send_sem, recv_sem) = scratch
    ext, halo, pack = (e0, e1, e2), (px0, px1, px2), (pk0, pk1, pk2)
    nz, ny, nx = counts
    gz, gy, gx = lax.axis_index("gz"), lax.axis_index("gy"), lax.axis_index("gx")

    def neighbour(step, sign):
        dz, dy, dx = (sign * s for s in step)
        z, y, x = gz + dz, gy + dy, gx + dx
        here = None
        for d, v, n in ((dz, z, nz), (dy, y, ny), (dx, x, nx)):
            test = v < n if d > 0 else (v >= 0 if d < 0 else None)
            if test is not None:
                here = test if here is None else here & test
        return here, {"gz": z, "gy": y, "gx": x}

    load = pltpu.make_async_copy(q_hbm, e0.at[pl.ds(8, 32), pl.ds(8, 32), :], local_sem)
    load.start()
    load_taps = pltpu.make_async_copy(taps_hbm, taps, taps_sem)
    load_taps.start()

    barrier = pltpu.get_barrier_semaphore()
    for step in STEPS:
        here, device = neighbour(step, 1)

        @pl.when(here)
        def _():
            pl.semaphore_signal(barrier, inc=1, device_id=device, device_id_type=MESH)

    def places(level, step):
        lv = LEVELS[level]
        dz, dy, dx = step
        if dx == 0:
            z, y = lv["z"][dz], lv["y"][dy]
            src = ext[level].at[pl.ds(z[0], z[2]), pl.ds(y[0], y[2]), :]
            dst = ext[level].at[pl.ds(z[1], z[2]), pl.ds(y[1], y[2]), :]
        else:
            face = 0 if dx == 1 else 1
            z, y = lv["pg"][dz], lv["py"][dy]
            src = pack[level].at[face, pl.ds(z[0], z[2]), pl.ds(y[0], y[2]), :]
            dst = halo[level].at[face, pl.ds(z[1], z[2]), pl.ds(y[1], y[2]), :]
        return src, dst

    for level in range(3):
        for step in STEPS:
            source, _ = neighbour(step, -1)
            _, dst = places(level, step)

            @pl.when(jnp.logical_not(source))
            def _():
                dst[...] = jnp.zeros(dst.shape, F32)

    def pack_faces(level):
        lv, src, width = LEVELS[level], ext[level], LEVELS[level]["width"]
        start, planes = lv["own"]
        lane = iota((lv["packrows"], 128), 1) // width
        for g, offset in enumerate(lv["groups"]):
            faces = [jnp.zeros((lv["packrows"], 128), F32) for _ in range(2)]
            for j in range(min(128 // width, planes - offset)):
                v = join([src[start + offset + j, r : r + n, :] for r, n in lv["tiles"]], 0)
                for f in range(2):
                    if level == 0:
                        faces[f] = pick(lane == j, pltpu.roll(v, (width * j - lv["face"][f]) % 128, 1), faces[f])
                if level == 1:
                    moved = pltpu.roll(v, (16 * j - 80) % 128, 1)
                    faces = [pick(lane == (j + 1 - f) % 8, moved, faces[f]) for f in range(2)]
            for f in range(2):
                pack[level][f, g] = faces[f]

    def copies(level, across):
        result = []
        for step in STEPS:
            if across is not None and (step[2] != 0) != across:
                continue
            target, device = neighbour(step, 1)
            src, dst = places(level, step)
            copy = pltpu.make_async_remote_copy(
                src_ref=src, dst_ref=dst, send_sem=send_sem.at[level, step[2] % 3], recv_sem=recv_sem.at[level, step[2] % 3],
                device_id=device, device_id_type=MESH)
            result.append((target, copy))
        return result

    def send(level, across):
        for target, copy in copies(level, across):
            @pl.when(target)
            def _():
                copy.start()

    def wait_all(level, semaphores, sign, kinds):
        places_z = (gz == 0, (gz > 0) & (gz < nz - 1), gz == nz - 1)
        places_y = (gy == 0, (gy > 0) & (gy < ny - 1), gy == ny - 1)
        for dx in kinds:
            side = {0: gx >= 0, 1: gx < nx - 1, -1: gx > 0}[sign * dx]
            for z, at_z in enumerate(places_z):
                for y, at_y in enumerate(places_y):
                    units = 0
                    for step in STEPS:
                        if step[2] == dx and 0 <= z + sign * step[0] <= 2 and 0 <= y + sign * step[1] <= 2:
                            shape = places(level, step)[1].shape
                            units += math.prod(shape) // 1024
                    whole = measure.at[pl.ds(0, units)]

                    @pl.when(at_z & at_y & side)
                    def _():
                        pltpu.make_async_copy(whole, whole, semaphores.at[level, dx % 3]).wait()

    def receive(level, across):
        wait_all(level, recv_sem, -1, {None: (0, 1, -1), False: (0,), True: (1, -1)}[across])

    def finish(level):
        wait_all(level, send_sem, 1, (0, 1, -1))

    def unpack_own(target):
        lane = iota((32, 128), 1)
        for first, count, _, _ in LEVELS[2]["runs"]:
            for e in range(first, first + count):
                place, shift = coarse_place(e)
                v = e2[place, 0:32, :]
                v = pltpu.roll(v, 128 - shift, 1) if shift else v
                target[e] = pick(lane < 64, v, pltpu.roll(v, 64, 1))

    def unpack(level, target):
        lv = LEVELS[level]
        rows, width = lv["keep"], lv["width"]
        lane = iota((rows, 128), 1)
        start = 34 if level == 2 else lv["hi"][0]
        here = lane % 64 if level == 2 else lane
        used = (here >= 37) & (here < 63) if level == 2 else (lane >= start) & (lane < start + 2 * width)
        even = (lane // width) % 2 == 0
        for first, count, g, j0 in lv["runs"]:
            leading, trailing = (halo[level][0, g], halo[level][1, g]) if level == 2 else (halo[level][1, g], halo[level][0, g])
            trailing = trailing if level else pltpu.roll(trailing, width, 1)
            pair = (pick(even, leading, trailing), pick(even, trailing, leading))
            places = range(8) if level == 2 else range(j0, j0 + count)
            moved = {j: pltpu.roll(pair[j % 2], (start - width * j) % 128, 1) for j in places}
            for i in range(count):
                e, j = first + i, j0 + i
                if level == 2:
                    target[e] = pick(used, pick(lane < 64, moved[j], moved[(j + 4) % 8]), target[e])
                else:
                    target[e] = pick(used, moved[j], 0.0 if level == 0 else ext[level][e, 0:rows, :])

    load.wait()
    pack_faces(0)
    reach = [1 + jnp.minimum(g, 1) + jnp.minimum(n - 1 - g, 1) for g, n in ((gz, nz), (gy, ny), (gx, nx))]
    pl.semaphore_wait(barrier, reach[0] * reach[1] * reach[2] - 1)
    send(0, False)
    send(0, True)

    load_taps.wait()

    def tap_row(level, term):
        return [taps[level, term, k] for k in range(17)]

    def tap_pair(level, second):
        return [jnp.where(second, taps[level, 1, k], taps[level, 0, k]) for k in range(17)]

    def inside(coord, g, n, count):
        return (coord + g * n >= 0) & (coord + g * n < n * count)

    for t in range(2):
        high, low = split(band(x_coords(iota((256, 128), 0), 0) - iota((256, 128), 1), tap_row(0, t)))
        cols = slice(128 * t, 128 * (t + 1))
        x0[0:256, cols], x0[256:512, cols], x0[512:768, cols] = high, high, low
    sq = (128, 128)
    row, col = iota(sq, 0), iota(sq, 1)
    m, c = col - 1, col - 2
    m = pick(col < 67, m, pick((col >= 80) & (col < 96), col - 81, pick((col >= 96) & (col < 112), col - 46, NOWHERE)))
    high = pick(inside(m, gx, 64, nx), weight(row - 2 * m), 0.0).astype(BF16)
    xr1[0:128], xr1[128:256] = high, high
    c = pick(col < 37, c, pick((col >= 48) & (col < 64), col - 29, pick((col >= 64) & (col < 80), col - 66, NOWHERE)))
    high = pick((row < 67) & inside(c, gx, 32, nx), weight(row - 1 - 2 * c), 0.0).astype(BF16)
    xr2[0:128], xr2[128:256] = high, high
    m_col, m_row, c_col, c_row = col - 1, row - 1, col - 2, row - 2
    up1 = pick(m_row < 66, weight(col - 2 * m_row), 0.0)
    up2 = pick((c_row < 35) & (m_col < 66) & inside(m_col, gx, 64, nx), weight(m_col - 2 * c_row), 0.0)
    up21 = exact(up2, up1)
    for t in range(2):
        k1 = pick((m_col < 66) & inside(m_col, gx, 64, nx), band(x_coords(row, 1) - m_col, tap_row(1, t)), 0.0)
        high, low = split(exact(k1, up1))
        for first, part in ((0, high), (256, high), (512, low)):
            x1[first + 128 * t : first + 128 * (t + 1)] = part
    k2 = band(x_coords(pick(row < 64, row, row - 64), 2) - c_col, tap_pair(2, row >= 64))
    k2 = pick((c_col < 35) & inside(c_col, gx, 32, nx), k2, 0.0)
    high, low = split(exact(k2, up21))
    x2[0:128], x2[128:256], x2[256:384] = high, high, low

    row, col = iota((32, 128), 0), iota((32, 128), 1)
    m = pick(row < 24, row - 2, row - 24 + 3)
    yr1[...] = pick((m < 19) & inside(m, gy, 16, ny), weight(y_coords(col, 0) - 2 * m), 0.0).astype(BF16)
    for t in range(2):
        y0[64 * t : 64 * t + 32], y0[64 * t + 32 : 64 * t + 64] = split(band(y_coords(col, 0) - row, tap_row(0, t)))
    m_col = col - 1
    yup1 = pick(m_col < 18, weight(row - 2 * m_col), 0.0)
    row, col = iota((24, 128), 0), iota((24, 128), 1)
    c = pick(row < 16, row - 3, row - 16 + 4)
    yr2[...] = pick((c < 12) & inside(c, gy, 8, ny), weight(y_coords(col, 1) - 2 * c), 0.0).astype(BF16)
    row, col = iota(sq, 0), iota(sq, 1)
    m_row, c_col, c_row = row - 1, col - 2, row - 2
    yup2 = pick((m_row < 18) & inside(m_row, gy, 16, ny) & (c_col < 11), weight(m_row - 2 * c_col), 0.0)
    yup21 = exact(yup1, yup2)
    for t in range(2):
        k1 = pick((m_row < 18) & inside(m_row, gy, 16, ny), band(y_coords(col, 1) - m_row, tap_row(1, t)), 0.0)
        y1[64 * t : 64 * t + 32], y1[64 * t + 32 : 64 * t + 64] = split(exact(yup1, k1))
        k2 = pick((c_row < 11) & inside(c_row, gy, 8, ny), band(y_coords(col, 2) - c_row, tap_row(2, t)), 0.0)
        y2[32 * t : 32 * t + 32], y2[64 + 32 * t : 96 + 32 * t] = split(exact(yup21, k2))

    z_low = jnp.where(gz > 0, 1.0, 0.0).astype(F32)
    z_high = jnp.where(gz < nz - 1, 1.0, 0.0).astype(F32)

    def edge(v, low, high):
        n = v.shape[0]
        return jnp.concatenate([v[:low] * z_low, v[low : n - high], v[n - high :] * z_high], axis=0)

    def pieces(v, count):
        return [v[:, 128 * i : 128 * (i + 1)] for i in range(count)]

    receive(0, False)

    def restrict_z(i, _):
        rows = pl.ds(pl.multiple_of(8 * i, 8), 8)
        even, odd = (jnp.concatenate([e0[2 * k + h : 2 * k + h + 1, rows, :] for k in range(24)], axis=0) for h in range(2))
        v = even[2:23] + 0.5625 * (odd[1:22] + odd[2:23]) - 0.0625 * (odd[0:21] + odd[3:24])
        r0[:, rows, :] = edge(v, 2, 3)
        return 0

    lax.fori_loop(0, 6, restrict_z, 0)
    for p in range(0, 21, 7):
        high, low = split(join([r0[p + i] for i in range(7)], 1))
        v = join(pieces(dot(yr1[:, 0:48], high) + dot(yr1[:, 0:48], low), 7), 0)
        v = dot(join(split(v), 1), xr1[...]).reshape(7, 32, 128)
        for i in range(7):
            e1[7 + p + i, 8:32, :] = v[i, 0:24]
            e1[7 + p + i, 40:48, :] = v[i, 24:32]
    send(1, False)
    pack_faces(1)
    send(1, True)
    receive(0, True)
    unpack(0, side)

    def conv_x0(i, _):
        planes = pl.ds(16 * i, 16)
        own_high, own_low = split(e0[planes].reshape(768, 128))
        side_high, side_low = split(side[planes].reshape(768, 128))
        left = join([own_high, side_high, own_low, side_low, own_high, side_high], 1)
        v = dot(left, x0[...])
        for t in range(2):
            f0[t, planes] = v[:, 128 * t : 128 * (t + 1)].reshape(16, 48, 128)
        return 0

    lax.fori_loop(0, 2, conv_x0, 0)

    finish(0)
    receive(1, False)

    def restrict_z1(i, _):
        rows = pl.ds(pl.multiple_of(8 * i, 8), 8)
        even = jnp.concatenate([e1[2 * k : 2 * k + 1, rows, :] for k in range(18)], axis=0)
        odd = jnp.concatenate([e1[2 * k + 1 : 2 * k + 2, rows, :] for k in range(17)], axis=0)
        v = odd[1:16] + 0.5625 * (even[1:16] + even[2:17]) - 0.0625 * (even[0:15] + even[3:18])
        r1[:, rows, :] = edge(v, 3, 4)
        return 0

    lax.fori_loop(0, 5, restrict_z1, 0)
    high, low = split(join([r1[p] for p in range(15)], 1))
    v = dot(yr2[:, 0:40], high) + dot(yr2[:, 0:40], low)
    v = dot(join(split(join(pieces(v, 15), 0)), 1), xr2[...]).reshape(15, 24, 128)
    place = iota((24, 128), 1) // 16
    for g, offset in enumerate(LEVELS[2]["groups"]):
        faces = [jnp.zeros((24, 128), F32) for _ in range(2)]
        for j in range(min(8, 15 - offset)):
            moved = pltpu.roll(v[offset + j], (16 * j - 48) % 128, 1)
            faces = [pick(place == (j + f) % 8, moved, faces[f]) for f in range(2)]
        for f in range(2):
            pk2[f, g] = faces[f]
    send(2, True)
    own = iota((24, 128), 1) < 37
    for g in range(6):
        w = None
        for k in range(3):
            p = 3 * g - 2 + k
            if 0 <= p < 15:
                part = pick(own, v[p], 0.0)
                part = pltpu.roll(part, 42 * k, 1) if k else part
                w = part if w is None else w + part
        e2[3 + g, 8:24, :] = w[0:16]
        e2[3 + g, 32:40, :] = w[16:24]
    send(2, False)

    lax.fori_loop(2, 3, conv_x0, 0)

    def fine_y(i, _):
        for t in range(2):
            high, low = split(join([f0[t, 6 * i + k] for k in range(6)], 1))
            matrix = y0[64 * t : 64 * t + 64, 0:48]
            both = dot(matrix, high)
            v = pieces(both[0:32] + both[32:64] + dot(matrix[0:32], low), 6)
            for k in range(6):
                s0[t, 6 * i + k] = v[k]
        return 0

    lax.fori_loop(0, 8, fine_y, 0)


    def conv_z(field, row, count):
        total = row[0] * field(0, count)
        for k in range(1, 17):
            total = total + row[k] * field(k, count)
        return total

    def conv_z0(i, _):
        rows = pl.ds(pl.multiple_of(8 * i, 8), 8)
        v = conv_z(lambda k, n: s0[0, k : k + n, rows, :], tap_row(0, 0), 32)
        v = v + conv_z(lambda k, n: s0[1, k : k + n, rows, :], tap_row(0, 1), 32)
        for k in range(32):
            out[k // 2, k % 2, rows, :] = v[k]
        return 0

    lax.fori_loop(0, 4, conv_z0, 0)

    receive(1, True)
    unpack(1, v1)

    def conv_z1(i, _):
        rows = pl.ds(pl.multiple_of(8 * i, 8), 8)
        for t in range(2):
            z1[t, :, rows, :] = edge(conv_z(lambda k, n: v1[k : k + n, rows, :], tap_row(1, t), 19), 1, 2)
        return 0

    lax.fori_loop(0, 5, conv_z1, 0)
    for t in range(2):
        for p, n in ((0, 7), (7, 6), (13, 6)):
            high, low = split(join([z1[t, p + i] for i in range(n)], 1))
            both = dot(y1[64 * t : 64 * t + 64, 0:40], high)
            v = both[0:32] + both[32:64] + dot(y1[64 * t : 64 * t + 32, 0:40], low)
            for i, piece in enumerate(pieces(v, n)):
                q1h[p + i, :, 128 * t : 128 * (t + 1)], q1l[p + i, :, 128 * t : 128 * (t + 1)] = split(piece)
    for p, n in ((0, 7), (7, 6), (13, 6)):
        high, low = (r[p : p + n].reshape(32 * n, 256) for r in (q1h, q1l))
        t1[p : p + n] = dot(join([high, low, high], 1), x1[...]).reshape(n, 32, 128)

    def refine(g, n):
        even = g[1 : n + 1]
        return even, 0.5625 * (even + g[2 : n + 2]) - 0.0625 * (g[0:n] + g[3 : n + 3])

    def add_middle(i, _):
        rows = pl.ds(pl.multiple_of(8 * i, 8), 8)
        for h, v in enumerate(refine(t1[:, rows, :], 16)):
            out[:, h, rows, :] = out[:, h, rows, :] + v
        return 0

    lax.fori_loop(0, 4, add_middle, 0)

    receive(2, False)
    unpack_own(v2)
    finish(1)
    finish(2)
    receive(2, True)
    unpack(2, v2)

    first_term = iota((8, 128), 1) < 64

    def conv_z2(i, _):
        rows = pl.ds(pl.multiple_of(8 * i, 8), 8)
        row = [v[None] for v in tap_pair(2, jnp.logical_not(first_term))]
        z2[:, rows, :] = edge(conv_z(lambda k, n: v2[k : k + n, rows, :], row, 13), 2, 3)
        return 0

    lax.fori_loop(0, 4, conv_z2, 0)
    lane = iota((32, 128), 1)
    for p, n in ((0, 7), (7, 6)):
        high, low = split(join([z2[p + i] for i in range(n)], 1))
        both, rest = dot(y2[:, 0:32], high), dot(y2[0:64, 0:32], low)
        terms = [pieces(both[32 * t : 32 * t + 32] + both[64 + 32 * t : 96 + 32 * t] + rest[32 * t : 32 * t + 32], n) for t in range(2)]
        high, low = split(join([pick(lane < 64, a, b) for a, b in zip(*terms)], 0))
        t2[p : p + n] = dot(join([high, low, high], 1), x2[...]).reshape(n, 32, 128)

    def add_coarse(i, _):
        rows = pl.ds(pl.multiple_of(8 * i, 8), 8)
        h = t2[:, rows, :]
        even = h[2:11]
        odd = 0.5625 * (h[1:11] + h[2:12]) - 0.0625 * (h[0:10] + h[3:13])
        g = []
        for k in range(9):
            g += [odd[k : k + 1], even[k : k + 1]]
        g = edge(jnp.concatenate(g + [odd[9:10]], axis=0), 1, 2)
        for h, v in enumerate(refine(g, 16)):
            out[:, h, rows, :] = out[:, h, rows, :] + v
        return 0

    lax.fori_loop(0, 4, add_coarse, 0)


def solution(mesh):
    counts = tuple(mesh.shape[a] for a in ("gz", "gy", "gx"))

    def local(charges, kernel_taps):
        vm = pltpu.VMEM
        scratch = [
            vm((48, 48, 128), F32), vm((35, 48, 128), F32), vm((12, 40, 128), F32),
            vm((2, 4, 48, 128), F32), vm((2, 5, 40, 128), F32), vm((2, 4, 32, 128), F32),
            vm((2, 2, 32, 128), F32), vm((2, 4, 32, 128), F32), vm((2, 3, 24, 128), F32),
            vm((48, 48, 128), F32), vm((35, 40, 128), F32), vm((29, 32, 128), F32),
            vm((21, 48, 128), F32), vm((15, 40, 128), F32), vm((2, 48, 48, 128), F32), vm((2, 48, 32, 128), F32),
            vm((2, 19, 40, 128), F32), vm((19, 32, 256), BF16), vm((19, 32, 256), BF16), vm((19, 32, 128), F32),
            vm((13, 32, 128), F32), vm((13, 32, 128), F32),
            vm((768, 256), BF16), vm((256, 128), BF16), vm((768, 128), BF16), vm((256, 128), BF16), vm((384, 128), BF16),
            vm((32, 128), BF16), vm((24, 128), BF16), vm((128, 128), BF16), vm((128, 128), BF16), vm((128, 128), BF16),
            pltpu.SMEM((3, 2, 17), F32),
            pltpu.SemaphoreType.DMA, pltpu.SemaphoreType.DMA, vm((160, 8, 128), F32), pltpu.SemaphoreType.DMA((3, 3)), pltpu.SemaphoreType.DMA((3, 3)),
        ]
        result = pl.pallas_call(
            functools.partial(kernel, counts),
            out_shape=jax.ShapeDtypeStruct((16, 2, 32, 128), F32),
            in_specs=[pl.BlockSpec(memory_space=pltpu.HBM)] * 2,
            out_specs=pl.BlockSpec(memory_space=pltpu.VMEM),
            scratch_shapes=scratch,
            compiler_params=pltpu.CompilerParams(
                collective_id=0, has_side_effects=True, vmem_limit_bytes=26 * 1024 * 1024),
        )(*(pltpu.with_memory_space_constraint(a, pltpu.HBM) for a in (charges, kernel_taps)))
        return result.reshape(32, 32, 128)

    return jax.shard_map(
        local, mesh=mesh, in_specs=(P("gz", "gy", "gx"), P()), out_specs=P("gz", "gy", "gx"), check_vma=False)
```

```python
import functools
import math

import jax
import jax.numpy as jnp
from jax import lax
from jax.experimental import pallas as pl
from jax.experimental.pallas import tpu as pltpu
from jax.sharding import PartitionSpec as P

F32, BF16 = jnp.float32, jnp.bfloat16
MESH = pl.DeviceIdType.MESH
NOWHERE = -10000

LEVELS = (
    dict(keep=48, own=(8, 32), z={0: (8, 8, 32), 1: (32, 0, 8), -1: (8, 40, 8)},
         y={0: (8, 8, 32), 1: (32, 0, 8), -1: (8, 40, 8)}, tiles=((8, 32),), packrows=32, groups=(0, 16), width=8,
         py={0: (0, 8, 32), 1: (24, 0, 8), -1: (0, 40, 8)}, pg={0: (0, 1, 2), 1: (1, 0, 1), -1: (0, 3, 1)},
         face=(120, 0), hi=(80, 8, 0), lo=(88, 8, 0), runs=((0, 8, 0, 8), (8, 16, 1, 0), (24, 16, 2, 0), (40, 8, 3, 0))),
    dict(keep=40, own=(7, 21), z={0: (7, 7, 21), 1: (16, 0, 7), -1: (12, 28, 7)},
         y={0: (8, 8, 24), 1: (16, 0, 8), -1: (40, 32, 8)}, tiles=((8, 24), (40, 8)), packrows=32, groups=(0, 8, 16, 4), width=16,
         py={0: (0, 8, 24), 1: (8, 0, 8), -1: (24, 32, 8)}, pg={0: (0, 1, 3), 1: (1, 0, 1), -1: (3, 4, 1)},
         face=(51, 0), hi=(80, 16, 0), lo=(96, 16, 0), runs=((0, 7, 0, 1), (7, 8, 1, 0), (15, 8, 2, 0), (23, 5, 3, 0), (28, 7, 4, 1))),
    dict(keep=32, own=(7, 15), z={0: (3, 3, 6), 1: (4, 0, 3), -1: (6, 9, 3)},
         y={0: (8, 8, 16), 1: (8, 0, 8), -1: (32, 24, 8)}, tiles=((8, 16), (32, 8)), packrows=24, groups=(0, 8, 7), width=16,
         py={0: (0, 8, 16), 1: (0, 0, 8), -1: (16, 24, 8)}, pg={0: (0, 1, 2), 1: (0, 0, 1), -1: (2, 3, 1)},
         face=(21, 0), hi=(50, 13, 0), lo=(37, 13, 3), runs=((0, 7, 0, 1), (7, 8, 1, 0), (15, 7, 2, 0), (22, 7, 3, 0))),
)
STEPS = tuple((dz, dy, dx) for xs in ((1, -1), (0,)) for dy in (1, -1, 0) for dz in (1, -1, 0) for dx in xs if (dz, dy, dx) != (0, 0, 0))


def coarse_place(e):
    if e < 7:
        return e // 3, 42 * (e % 3)
    if e < 22:
        return 3 + (e - 5) // 3, 42 * ((e - 5) % 3)
    return 9 + (e - 22) // 3, 42 * ((e - 22) % 3)


def split(x):
    high = x.astype(BF16)
    return high, (x - high.astype(F32)).astype(BF16)


def iota(shape, axis):
    return lax.broadcasted_iota(jnp.int32, shape, axis)


def pick(condition, value, other):
    return jnp.where(condition, value, other)


def dot(a, b):
    return jnp.dot(a, b, preferred_element_type=F32)


def join(parts, axis):
    return parts[0] if len(parts) == 1 else jnp.concatenate(parts, axis=axis)


def exact(a, b):
    return jnp.dot(a, b, preferred_element_type=F32, precision=lax.Precision.HIGHEST)


def weight(d):
    d = jnp.abs(d)
    return pick(d == 0, 1.0, pick(d == 1, 0.5625, pick(d == 3, -0.0625, 0.0))).astype(F32)


def band(diff, row):
    total = jnp.zeros(diff.shape, F32)
    for k in range(17):
        total = pick(diff == k - 8, row[k], total)
    return total


def x_coords(slot, level):
    base, first, high, low, tile = ((128, 0, 128, -8, 128), (67, -1, 63, -14, 0), (37, -2, 30, -10, 0))[level]
    coord = pick(slot < base, slot + first, NOWHERE)
    for (start, count, _), value in ((LEVELS[level]["hi"], high), (LEVELS[level]["lo"], low)):
        k = slot - tile - start
        coord = pick((k >= 0) & (k < count), k + value, coord)
    return coord


def y_coords(row, level):
    if level == 0:
        return row - 8
    if level == 1:
        coord = pick(row < 8, row - 10, pick(row < 29, row - 10, NOWHERE))
        return pick((row >= 32) & (row < 40), row - 32 + 19, coord)
    coord = pick(row < 8, row - 11, pick(row < 23, row - 11, NOWHERE))
    return pick((row >= 24) & (row < 32), row - 24 + 12, coord)


def kernel(counts, q_hbm, taps_hbm, out, *scratch):
    (e0, e1, e2, px0, px1, px2, pk0, pk1, pk2, side, v1, v2, r0, r1, f0, s0, z1, q1h, q1l, t1, z2, t2,
     x0, xr1, x1, xr2, x2, yr1, yr2, y0, y1, y2, taps, local_sem, taps_sem, measure, send_sem, recv_sem) = scratch
    ext, halo, pack = (e0, e1, e2), (px0, px1, px2), (pk0, pk1, pk2)
    nz, ny, nx = counts
    gz, gy, gx = lax.axis_index("gz"), lax.axis_index("gy"), lax.axis_index("gx")

    def neighbour(step, sign):
        dz, dy, dx = (sign * s for s in step)
        z, y, x = gz + dz, gy + dy, gx + dx
        here = None
        for d, v, n in ((dz, z, nz), (dy, y, ny), (dx, x, nx)):
            test = v < n if d > 0 else (v >= 0 if d < 0 else None)
            if test is not None:
                here = test if here is None else here & test
        return here, {"gz": z, "gy": y, "gx": x}

    load = pltpu.make_async_copy(q_hbm, e0.at[pl.ds(8, 32), pl.ds(8, 32), :], local_sem)
    load.start()
    load_taps = pltpu.make_async_copy(taps_hbm, taps, taps_sem)
    load_taps.start()

    barrier = pltpu.get_barrier_semaphore()
    for step in STEPS:
        here, device = neighbour(step, 1)

        @pl.when(here)
        def _():
            pl.semaphore_signal(barrier, inc=1, device_id=device, device_id_type=MESH)

    def places(level, step):
        lv = LEVELS[level]
        dz, dy, dx = step
        if dx == 0:
            z, y = lv["z"][dz], lv["y"][dy]
            src = ext[level].at[pl.ds(z[0], z[2]), pl.ds(y[0], y[2]), :]
            dst = ext[level].at[pl.ds(z[1], z[2]), pl.ds(y[1], y[2]), :]
        else:
            face = 0 if dx == 1 else 1
            z, y = lv["pg"][dz], lv["py"][dy]
            src = pack[level].at[face, pl.ds(z[0], z[2]), pl.ds(y[0], y[2]), :]
            dst = halo[level].at[face, pl.ds(z[1], z[2]), pl.ds(y[1], y[2]), :]
        return src, dst

    for level in range(3):
        for step in STEPS:
            source, _ = neighbour(step, -1)
            _, dst = places(level, step)

            @pl.when(jnp.logical_not(source))
            def _():
                dst[...] = jnp.zeros(dst.shape, F32)

    def pack_faces(level):
        lv, src, width = LEVELS[level], ext[level], LEVELS[level]["width"]
        start, planes = lv["own"]
        lane = iota((lv["packrows"], 128), 1) // width
        for g, offset in enumerate(lv["groups"]):
            faces = [jnp.zeros((lv["packrows"], 128), F32) for _ in range(2)]
            for j in range(min(128 // width, planes - offset)):
                v = join([src[start + offset + j, r : r + n, :] for r, n in lv["tiles"]], 0)
                for f in range(2):
                    if level == 0:
                        faces[f] = pick(lane == j, pltpu.roll(v, (width * j - lv["face"][f]) % 128, 1), faces[f])
                if level == 1:
                    moved = pltpu.roll(v, (16 * j - 80) % 128, 1)
                    faces = [pick(lane == (j + 1 - f) % 8, moved, faces[f]) for f in range(2)]
            for f in range(2):
                pack[level][f, g] = faces[f]

    def copies(level, across):
        result = []
        for step in STEPS:
            if across is not None and (step[2] != 0) != across:
                continue
            target, device = neighbour(step, 1)
            src, dst = places(level, step)
            copy = pltpu.make_async_remote_copy(
                src_ref=src, dst_ref=dst, send_sem=send_sem.at[level, step[2] % 3], recv_sem=recv_sem.at[level, step[2] % 3],
                device_id=device, device_id_type=MESH)
            result.append((target, copy))
        return result

    def send(level, across):
        for target, copy in copies(level, across):
            @pl.when(target)
            def _():
                copy.start()

    def wait_all(level, semaphores, sign, kinds):
        places_z = (gz == 0, (gz > 0) & (gz < nz - 1), gz == nz - 1)
        places_y = (gy == 0, (gy > 0) & (gy < ny - 1), gy == ny - 1)
        for dx in kinds:
            side = {0: gx >= 0, 1: gx < nx - 1, -1: gx > 0}[sign * dx]
            for z, at_z in enumerate(places_z):
                for y, at_y in enumerate(places_y):
                    units = 0
                    for step in STEPS:
                        if step[2] == dx and 0 <= z + sign * step[0] <= 2 and 0 <= y + sign * step[1] <= 2:
                            shape = places(level, step)[1].shape
                            units += math.prod(shape) // 1024
                    whole = measure.at[pl.ds(0, units)]

                    @pl.when(at_z & at_y & side)
                    def _():
                        pltpu.make_async_copy(whole, whole, semaphores.at[level, dx % 3]).wait()

    def receive(level, across):
        wait_all(level, recv_sem, -1, {None: (0, 1, -1), False: (0,), True: (1, -1)}[across])

    def finish(level):
        wait_all(level, send_sem, 1, (0, 1, -1))

    def unpack_own(target):
        lane = iota((32, 128), 1)
        for first, count, _, _ in LEVELS[2]["runs"]:
            for e in range(first, first + count):
                place, shift = coarse_place(e)
                v = e2[place, 0:32, :]
                v = pltpu.roll(v, 128 - shift, 1) if shift else v
                target[e] = pick(lane < 64, v, pltpu.roll(v, 64, 1))

    def unpack(level, target):
        lv = LEVELS[level]
        rows, width = lv["keep"], lv["width"]
        lane = iota((rows, 128), 1)
        start = 34 if level == 2 else lv["hi"][0]
        here = lane % 64 if level == 2 else lane
        used = (here >= 37) & (here < 63) if level == 2 else (lane >= start) & (lane < start + 2 * width)
        even = (lane // width) % 2 == 0
        for first, count, g, j0 in lv["runs"]:
            leading, trailing = (halo[level][0, g], halo[level][1, g]) if level == 2 else (halo[level][1, g], halo[level][0, g])
            trailing = trailing if level else pltpu.roll(trailing, width, 1)
            pair = (pick(even, leading, trailing), pick(even, trailing, leading))
            places = range(8) if level == 2 else range(j0, j0 + count)
            moved = {j: pltpu.roll(pair[j % 2], (start - width * j) % 128, 1) for j in places}
            for i in range(count):
                e, j = first + i, j0 + i
                if level == 2:
                    target[e] = pick(used, pick(lane < 64, moved[j], moved[(j + 4) % 8]), target[e])
                else:
                    target[e] = pick(used, moved[j], 0.0 if level == 0 else ext[level][e, 0:rows, :])

    load.wait()
    pack_faces(0)
    reach = [1 + jnp.minimum(g, 1) + jnp.minimum(n - 1 - g, 1) for g, n in ((gz, nz), (gy, ny), (gx, nx))]
    pl.semaphore_wait(barrier, reach[0] * reach[1] * reach[2] - 1)
    send(0, False)
    send(0, True)

    load_taps.wait()

    def tap_row(level, term):
        return [taps[level, term, k] for k in range(17)]

    def tap_pair(level, second):
        return [jnp.where(second, taps[level, 1, k], taps[level, 0, k]) for k in range(17)]

    def inside(coord, g, n, count):
        return (coord + g * n >= 0) & (coord + g * n < n * count)

    for t in range(2):
        high, low = split(band(x_coords(iota((256, 128), 0), 0) - iota((256, 128), 1), tap_row(0, t)))
        cols = slice(128 * t, 128 * (t + 1))
        x0[0:256, cols], x0[256:512, cols], x0[512:768, cols] = high, high, low
    sq = (128, 128)
    row, col = iota(sq, 0), iota(sq, 1)
    m, c = col - 1, col - 2
    m = pick(col < 67, m, pick((col >= 80) & (col < 96), col - 81, pick((col >= 96) & (col < 112), col - 46, NOWHERE)))
    high = pick(inside(m, gx, 64, nx), weight(row - 2 * m), 0.0).astype(BF16)
    xr1[0:128], xr1[128:256] = high, high
    c = pick(col < 37, c, pick((col >= 48) & (col < 64), col - 29, pick((col >= 64) & (col < 80), col - 66, NOWHERE)))
    high = pick((row < 67) & inside(c, gx, 32, nx), weight(row - 1 - 2 * c), 0.0).astype(BF16)
    xr2[0:128], xr2[128:256] = high, high
    m_col, m_row, c_col, c_row = col - 1, row - 1, col - 2, row - 2
    up1 = pick(m_row < 66, weight(col - 2 * m_row), 0.0)
    up2 = pick((c_row < 35) & (m_col < 66) & inside(m_col, gx, 64, nx), weight(m_col - 2 * c_row), 0.0)
    up21 = exact(up2, up1)
    for t in range(2):
        k1 = pick((m_col < 66) & inside(m_col, gx, 64, nx), band(x_coords(row, 1) - m_col, tap_row(1, t)), 0.0)
        high, low = split(exact(k1, up1))
        for first, part in ((0, high), (256, high), (512, low)):
            x1[first + 128 * t : first + 128 * (t + 1)] = part
    k2 = band(x_coords(pick(row < 64, row, row - 64), 2) - c_col, tap_pair(2, row >= 64))
    k2 = pick((c_col < 35) & inside(c_col, gx, 32, nx), k2, 0.0)
    high, low = split(exact(k2, up21))
    x2[0:128], x2[128:256], x2[256:384] = high, high, low

    row, col = iota((32, 128), 0), iota((32, 128), 1)
    m = pick(row < 24, row - 2, row - 24 + 3)
    yr1[...] = pick((m < 19) & inside(m, gy, 16, ny), weight(y_coords(col, 0) - 2 * m), 0.0).astype(BF16)
    for t in range(2):
        y0[64 * t : 64 * t + 32], y0[64 * t + 32 : 64 * t + 64] = split(band(y_coords(col, 0) - row, tap_row(0, t)))
    m_col = col - 1
    yup1 = pick(m_col < 18, weight(row - 2 * m_col), 0.0)
    row, col = iota((24, 128), 0), iota((24, 128), 1)
    c = pick(row < 16, row - 3, row - 16 + 4)
    yr2[...] = pick((c < 12) & inside(c, gy, 8, ny), weight(y_coords(col, 1) - 2 * c), 0.0).astype(BF16)
    row, col = iota(sq, 0), iota(sq, 1)
    m_row, c_col, c_row = row - 1, col - 2, row - 2
    yup2 = pick((m_row < 18) & inside(m_row, gy, 16, ny) & (c_col < 11), weight(m_row - 2 * c_col), 0.0)
    yup21 = exact(yup1, yup2)
    for t in range(2):
        k1 = pick((m_row < 18) & inside(m_row, gy, 16, ny), band(y_coords(col, 1) - m_row, tap_row(1, t)), 0.0)
        y1[64 * t : 64 * t + 32], y1[64 * t + 32 : 64 * t + 64] = split(exact(yup1, k1))
        k2 = pick((c_row < 11) & inside(c_row, gy, 8, ny), band(y_coords(col, 2) - c_row, tap_row(2, t)), 0.0)
        y2[32 * t : 32 * t + 32], y2[64 + 32 * t : 96 + 32 * t] = split(exact(yup21, k2))

    z_low = jnp.where(gz > 0, 1.0, 0.0).astype(F32)
    z_high = jnp.where(gz < nz - 1, 1.0, 0.0).astype(F32)

    def edge(v, low, high):
        n = v.shape[0]
        return jnp.concatenate([v[:low] * z_low, v[low : n - high], v[n - high :] * z_high], axis=0)

    def pieces(v, count):
        return [v[:, 128 * i : 128 * (i + 1)] for i in range(count)]

    receive(0, False)

    def restrict_z(i, _):
        rows = pl.ds(pl.multiple_of(8 * i, 8), 8)
        even, odd = (jnp.concatenate([e0[2 * k + h : 2 * k + h + 1, rows, :] for k in range(24)], axis=0) for h in range(2))
        v = even[2:23] + 0.5625 * (odd[1:22] + odd[2:23]) - 0.0625 * (odd[0:21] + odd[3:24])
        r0[:, rows, :] = edge(v, 2, 3)
        return 0

    lax.fori_loop(0, 6, restrict_z, 0)
    for p in range(0, 21, 7):
        high, low = split(join([r0[p + i] for i in range(7)], 1))
        v = join(pieces(dot(yr1[:, 0:48], high) + dot(yr1[:, 0:48], low), 7), 0)
        v = dot(join(split(v), 1), xr1[...]).reshape(7, 32, 128)
        for i in range(7):
            e1[7 + p + i, 8:32, :] = v[i, 0:24]
            e1[7 + p + i, 40:48, :] = v[i, 24:32]
    send(1, False)
    pack_faces(1)
    send(1, True)
    receive(0, True)
    unpack(0, side)

    def conv_x0(i, _):
        planes = pl.ds(16 * i, 16)
        own_high, own_low = split(e0[planes].reshape(768, 128))
        side_high, side_low = split(side[planes].reshape(768, 128))
        left = join([own_high, side_high, own_low, side_low, own_high, side_high], 1)
        v = dot(left, x0[...])
        for t in range(2):
            f0[t, planes] = v[:, 128 * t : 128 * (t + 1)].reshape(16, 48, 128)
        return 0

    lax.fori_loop(0, 2, conv_x0, 0)

    finish(0)
    receive(1, False)

    def restrict_z1(i, _):
        rows = pl.ds(pl.multiple_of(8 * i, 8), 8)
        even = jnp.concatenate([e1[2 * k : 2 * k + 1, rows, :] for k in range(18)], axis=0)
        odd = jnp.concatenate([e1[2 * k + 1 : 2 * k + 2, rows, :] for k in range(17)], axis=0)
        v = odd[1:16] + 0.5625 * (even[1:16] + even[2:17]) - 0.0625 * (even[0:15] + even[3:18])
        r1[:, rows, :] = edge(v, 3, 4)
        return 0

    lax.fori_loop(0, 5, restrict_z1, 0)
    high, low = split(join([r1[p] for p in range(15)], 1))
    v = dot(yr2[:, 0:40], high) + dot(yr2[:, 0:40], low)
    v = dot(join(split(join(pieces(v, 15), 0)), 1), xr2[...]).reshape(15, 24, 128)
    place = iota((24, 128), 1) // 16
    for g, offset in enumerate(LEVELS[2]["groups"]):
        faces = [jnp.zeros((24, 128), F32) for _ in range(2)]
        for j in range(min(8, 15 - offset)):
            moved = pltpu.roll(v[offset + j], (16 * j - 48) % 128, 1)
            faces = [pick(place == (j + f) % 8, moved, faces[f]) for f in range(2)]
        for f in range(2):
            pk2[f, g] = faces[f]
    send(2, True)
    own = iota((24, 128), 1) < 37
    for g in range(6):
        w = None
        for k in range(3):
            p = 3 * g - 2 + k
            if 0 <= p < 15:
                part = pick(own, v[p], 0.0)
                part = pltpu.roll(part, 42 * k, 1) if k else part
                w = part if w is None else w + part
        e2[3 + g, 8:24, :] = w[0:16]
        e2[3 + g, 32:40, :] = w[16:24]
    send(2, False)

    lax.fori_loop(2, 3, conv_x0, 0)

    def fine_y(i, _):
        for t in range(2):
            high, low = split(join([f0[t, 6 * i + k] for k in range(6)], 1))
            matrix = y0[64 * t : 64 * t + 64, 0:48]
            both = dot(matrix, high)
            v = pieces(both[0:32] + both[32:64] + dot(matrix[0:32], low), 6)
            for k in range(6):
                s0[t, 6 * i + k] = v[k]
        return 0

    lax.fori_loop(0, 8, fine_y, 0)


    def conv_z(field, row, count):
        total = row[0] * field(0, count)
        for k in range(1, 17):
            total = total + row[k] * field(k, count)
        return total

    def conv_z0(i, _):
        rows = pl.ds(pl.multiple_of(8 * i, 8), 8)
        v = conv_z(lambda k, n: s0[0, k : k + n, rows, :], tap_row(0, 0), 32)
        v = v + conv_z(lambda k, n: s0[1, k : k + n, rows, :], tap_row(0, 1), 32)
        for k in range(32):
            out[k // 2, k % 2, rows, :] = v[k]
        return 0

    lax.fori_loop(0, 4, conv_z0, 0)

    receive(1, True)
    unpack(1, v1)

    def conv_z1(i, _):
        rows = pl.ds(pl.multiple_of(8 * i, 8), 8)
        for t in range(2):
            z1[t, :, rows, :] = edge(conv_z(lambda k, n: v1[k : k + n, rows, :], tap_row(1, t), 19), 1, 2)
        return 0

    lax.fori_loop(0, 5, conv_z1, 0)
    for t in range(2):
        for p, n in ((0, 7), (7, 6), (13, 6)):
            high, low = split(join([z1[t, p + i] for i in range(n)], 1))
            both = dot(y1[64 * t : 64 * t + 64, 0:40], high)
            v = both[0:32] + both[32:64] + dot(y1[64 * t : 64 * t + 32, 0:40], low)
            for i, piece in enumerate(pieces(v, n)):
                q1h[p + i, :, 128 * t : 128 * (t + 1)], q1l[p + i, :, 128 * t : 128 * (t + 1)] = split(piece)
    for p, n in ((0, 7), (7, 6), (13, 6)):
        high, low = (r[p : p + n].reshape(32 * n, 256) for r in (q1h, q1l))
        t1[p : p + n] = dot(join([high, low, high], 1), x1[...]).reshape(n, 32, 128)

    def refine(g, n):
        even = g[1 : n + 1]
        return even, 0.5625 * (even + g[2 : n + 2]) - 0.0625 * (g[0:n] + g[3 : n + 3])

    def add_middle(i, _):
        rows = pl.ds(pl.multiple_of(8 * i, 8), 8)
        for h, v in enumerate(refine(t1[:, rows, :], 16)):
            out[:, h, rows, :] = out[:, h, rows, :] + v
        return 0

    lax.fori_loop(0, 4, add_middle, 0)

    receive(2, False)
    unpack_own(v2)
    finish(1)
    finish(2)
    receive(2, True)
    unpack(2, v2)

    first_term = iota((8, 128), 1) < 64

    def conv_z2(i, _):
        rows = pl.ds(pl.multiple_of(8 * i, 8), 8)
        row = [v[None] for v in tap_pair(2, jnp.logical_not(first_term))]
        z2[:, rows, :] = edge(conv_z(lambda k, n: v2[k : k + n, rows, :], row, 13), 2, 3)
        return 0

    lax.fori_loop(0, 4, conv_z2, 0)
    lane = iota((32, 128), 1)
    for p, n in ((0, 7), (7, 6)):
        high, low = split(join([z2[p + i] for i in range(n)], 1))
        both, rest = dot(y2[:, 0:32], high), dot(y2[0:64, 0:32], low)
        terms = [pieces(both[32 * t : 32 * t + 32] + both[64 + 32 * t : 96 + 32 * t] + rest[32 * t : 32 * t + 32], n) for t in range(2)]
        high, low = split(join([pick(lane < 64, a, b) for a, b in zip(*terms)], 0))
        t2[p : p + n] = dot(join([high, low, high], 1), x2[...]).reshape(n, 32, 128)

    def add_coarse(i, _):
        rows = pl.ds(pl.multiple_of(8 * i, 8), 8)
        h = t2[:, rows, :]
        even = h[2:11]
        odd = 0.5625 * (h[1:11] + h[2:12]) - 0.0625 * (h[0:10] + h[3:13])
        g = []
        for k in range(9):
            g += [odd[k : k + 1], even[k : k + 1]]
        g = edge(jnp.concatenate(g + [odd[9:10]], axis=0), 1, 2)
        for h, v in enumerate(refine(g, 16)):
            out[:, h, rows, :] = out[:, h, rows, :] + v
        return 0

    lax.fori_loop(0, 4, add_coarse, 0)


def solution(mesh):
    counts = tuple(mesh.shape[a] for a in ("gz", "gy", "gx"))

    def local(charges, kernel_taps):
        vm = pltpu.VMEM
        scratch = [
            vm((48, 48, 128), F32), vm((35, 48, 128), F32), vm((12, 40, 128), F32),
            vm((2, 4, 48, 128), F32), vm((2, 5, 40, 128), F32), vm((2, 4, 32, 128), F32),
            vm((2, 2, 32, 128), F32), vm((2, 4, 32, 128), F32), vm((2, 3, 24, 128), F32),
            vm((48, 48, 128), F32), vm((35, 40, 128), F32), vm((29, 32, 128), F32),
            vm((21, 48, 128), F32), vm((15, 40, 128), F32), vm((2, 48, 48, 128), F32), vm((2, 48, 32, 128), F32),
            vm((2, 19, 40, 128), F32), vm((19, 32, 256), BF16), vm((19, 32, 256), BF16), vm((19, 32, 128), F32),
            vm((13, 32, 128), F32), vm((13, 32, 128), F32),
            vm((768, 256), BF16), vm((256, 128), BF16), vm((768, 128), BF16), vm((256, 128), BF16), vm((384, 128), BF16),
            vm((32, 128), BF16), vm((24, 128), BF16), vm((128, 128), BF16), vm((128, 128), BF16), vm((128, 128), BF16),
            pltpu.SMEM((3, 2, 17), F32),
            pltpu.SemaphoreType.DMA, pltpu.SemaphoreType.DMA, vm((160, 8, 128), F32), pltpu.SemaphoreType.DMA((3, 3)), pltpu.SemaphoreType.DMA((3, 3)),
        ]
        result = pl.pallas_call(
            functools.partial(kernel, counts),
            out_shape=jax.ShapeDtypeStruct((16, 2, 32, 128), F32),
            in_specs=[pl.BlockSpec(memory_space=pltpu.HBM)] * 2,
            out_specs=pl.BlockSpec(memory_space=pltpu.VMEM),
            scratch_shapes=scratch,
            compiler_params=pltpu.CompilerParams(
                collective_id=0, has_side_effects=True, vmem_limit_bytes=26 * 1024 * 1024),
        )(*(pltpu.with_memory_space_constraint(a, pltpu.HBM) for a in (charges, kernel_taps)))
        return result.reshape(32, 32, 128)

    return jax.shard_map(
        local, mesh=mesh, in_specs=(P("gz", "gy", "gx"), P()), out_specs=P("gz", "gy", "gx"), check_vma=False)
```
